256 devices in a mesh: gx: 8 (over x, core), gy: 32 (over z, y).
Axes of the slice: x: 4, y: 4, z: 8, core: 2. Of those that a mesh axis runs over, the one named last changes fastest.
Arguments:
- source: bfloat16 [16, 4096, 256], P(None, ('gx', 'gy')), may hold values from -6 to 6
- leaf_flux: bfloat16 [262144, 256], P(('gx', 'gy')), may hold values from -0.375 to 0.375
- leaf_particular: bfloat16 [1048576, 256], P(('gx', 'gy')), may hold values from -0.375 to 0.375
- leaf_lift: bfloat16 [262144, 256], P(('gx', 'gy')), may hold values from -0.75 to 0.75
- box_up: bfloat16 [163840, 1024], P(('gx', 'gy')), may hold values from -0.1875 to 0.1875
- box_down: bfloat16 [262144, 640], P(('gx', 'gy')), may hold values from -0.25 to 0.25
- up_one: bfloat16 [65536, 768], P(('gx', 'gy')), may hold values from -0.1875 to 0.1875
- down_one: bfloat16 [65536, 768], P(('gx', 'gy')), may hold values from -0.21875 to 0.21875
- up_two: bfloat16 [32768, 1536], P(('gx', 'gy')), may hold values from -0.125 to 0.125
- down_two: bfloat16 [32768, 1536], P(('gx', 'gy')), may hold values from -0.15625 to 0.15625
- up_root: bfloat16 [16384, 6144], P(('gx', 'gy')), may hold values from -0.046875 to 0.046875
- down_root: bfloat16 [16384, 6144], P(('gx', 'gy')), may hold values from -0.078125 to 0.078125
Outputs:
- solution: float32 [16, 4096, 256], P(None, ('gx', 'gy'))
The draws below stay inside these ranges and needn't reach their ends.
All inputs are finite; a program needn't handle non-finite values.
Results may differ from the reference program's by a relative error of at most 0.014.
Values may be sent and summed in bfloat16 or wider, within the bound.
A program may use at most 64 MiB of HBM per device.

```python
import jax
import jax.numpy as jnp
from jax import lax

R = 16
Q = 256
EDGE = 64
LEAF = 16
K0 = 256
I0 = 384
Z0 = 640
K1 = 512
Z1 = 768
K2 = 1024
Z2 = 1536
NROOT = 16
IR = 6144
NLEAF = 4096
N_GX = 8
N_GY = 32


def block_scale(key, extent, shards, low, top_value):
    gain = 1.0
    for position, shards_of in shards:
        draws = jax.random.uniform(jax.random.fold_in(jax.random.fold_in(key, 6), position), (shards_of,), jnp.float32, low / len(shards), top_value / len(shards))
        gain = gain * jnp.repeat(jnp.exp(draws), extent[position] // shards_of).reshape((-1,) + (1,) * (len(extent) - 1 - position))
    return gain


def scatter_about(key, dims, deviation, most, cuts=(), kind=jnp.bfloat16):
    array = jax.random.normal(key, dims, jnp.float32) * deviation
    if len(cuts) > 0:
        array = block_scale(key, dims, cuts, -0.22, 0.18) * array
    return jnp.clip(array, min=-most, max=most).astype(kind)


def setup_inputs(seed: int = 0) -> dict:
    streams_of = jax.random.split(jax.random.key(seed), 13)
    source = scatter_about(streams_of[0], (R, NLEAF, Q), 1.0, 6.0, ((1, 256),))
    leaf_flux = scatter_about(streams_of[1], (NLEAF * EDGE, Q), Q ** -0.5, 0.375, ((0, 256),))
    leaf_particular = scatter_about(streams_of[2], (NLEAF * Q, Q), Q ** -0.5, 0.375, ((0, 256),))
    leaf_lift = scatter_about(streams_of[3], (NLEAF * EDGE, Q), EDGE ** -0.5, 0.75, ((0, 256),))
    box_up = scatter_about(streams_of[4], (N_GX * N_GY * Z0, LEAF * EDGE), (LEAF * EDGE) ** -0.5, 0.1875, ((0, 256),))
    box_down = scatter_about(streams_of[5], (N_GX * N_GY * LEAF * EDGE, Z0), Z0 ** -0.5, 0.25, ((0, 256),))
    up_one = scatter_about(streams_of[6], (N_GX * N_GY * K0, Z1), (4 * K0) ** -0.5, 0.1875, ((0, 256),))
    down_one = scatter_about(streams_of[7], (N_GX * N_GY * K0, Z1), Z1 ** -0.5, 0.21875, ((0, 256),))
    up_two = scatter_about(streams_of[8], (N_GX * N_GY * K1 // 4, Z2), (4 * K1) ** -0.5, 0.125, ((0, 256),))
    down_two = scatter_about(streams_of[9], (N_GX * N_GY * K1 // 4, Z2), Z2 ** -0.5, 0.15625, ((0, 256),))
    up_root = scatter_about(streams_of[10], (N_GX * N_GY * K2 // 16, IR), (NROOT * K2) ** -0.5, 0.046875, ((0, 256),))
    down_root = scatter_about(streams_of[11], (N_GX * N_GY * K2 // 16, IR), IR ** -0.5, 0.078125, ((0, 256),))
    return dict(source=source, leaf_flux=leaf_flux, leaf_particular=leaf_particular, leaf_lift=leaf_lift, box_up=box_up, box_down=box_down, up_one=up_one, down_one=down_one, up_two=up_two, down_two=down_two, up_root=up_root, down_root=down_root)


def batched(form, left, right):
    return jnp.einsum(form, left.astype(jnp.float32), right.astype(jnp.float32), precision=lax.Precision.HIGHEST)


def reference(source, leaf_flux, leaf_particular, leaf_lift, box_up, box_down, up_one, down_one, up_two, down_two, up_root, down_root):
    count = N_GX * N_GY
    sources = source.reshape(R, count, LEAF, Q)
    flux = batched("rdlq,dleq->drle", sources, leaf_flux.reshape(count, LEAF, EDGE, Q))
    flux = flux.astype(jnp.bfloat16).reshape(count, R, LEAF * EDGE)
    box_state = batched("drk,dzk->drz", flux, box_up.reshape(count, Z0, LEAF * EDGE)).astype(jnp.bfloat16)
    first_terms = batched("drk,dkz->drz", box_state[:, :, I0:], up_one.reshape(count, K0, Z1))
    first_state = jnp.sum(first_terms.reshape(count // 4, 4, R, Z1), axis=1).astype(jnp.bfloat16)
    second_terms = batched("crk,ckz->crz", first_state[:, :, K0:], up_two.reshape(count // 4, K1, Z2))
    second_state = jnp.sum(second_terms.reshape(count // 16, 4, R, Z2), axis=1).astype(jnp.bfloat16)
    root_state = batched("crk,cki->ri", second_state[:, :, K1:], up_root.reshape(count // 16, K2, IR)).astype(jnp.bfloat16)
    top_bound = batched("ri,cki->crk", root_state, down_root.reshape(count // 16, K2, IR)).astype(jnp.bfloat16)
    second_input = jnp.concatenate([second_state[:, :, :K1], top_bound], axis=2)
    mid_bound = batched("prz,pckz->pcrk", second_input, down_two.reshape(count // 16, 4, K1, Z2))
    mid_bound = mid_bound.astype(jnp.bfloat16).reshape(count // 4, R, K1)
    first_input = jnp.concatenate([first_state[:, :, :K0], mid_bound], axis=2)
    box_bound = batched("prz,pckz->pcrk", first_input, down_one.reshape(count // 4, 4, K0, Z1))
    box_bound = box_bound.astype(jnp.bfloat16).reshape(count, R, K0)
    box_input = jnp.concatenate([box_state[:, :, :I0], box_bound], axis=2)
    leaf_bound = batched("drz,dkz->drk", box_input, box_down.reshape(count, LEAF * EDGE, Z0))
    leaf_bound = leaf_bound.astype(jnp.bfloat16).reshape(count, R, LEAF, EDGE)
    lifted = batched("drle,dleq->rdlq", leaf_bound, leaf_lift.reshape(count, LEAF, EDGE, Q))
    particular = batched("rdlq,dlqp->rdlp", sources, leaf_particular.reshape(count, LEAF, Q, Q))
    return (lifted + particular).reshape(R, count * LEAF, Q)
```

```python
import jax
import jax.numpy as jnp
from jax import lax
from jax.experimental import pallas as pl
from jax.experimental.pallas import tpu as pltpu
from jax.sharding import PartitionSpec as P

MESH = pl.DeviceIdType.MESH
BF = jnp.bfloat16
F32 = jnp.float32

R = 16
LEAF = 16
ST_A, ST_AI, ST_B, ST_BI, ST_B2, ST_C1, ST_C2, ST_C3, ST_D, ST_E = range(10)
N_STAGE = 10


def nt(x, w):
    return lax.dot_general(x, w, (((1,), (1,)), ((), ())), preferred_element_type=F32)


def nn(x, w):
    return jnp.dot(x, w, preferred_element_type=F32)


def kernel(
    src_h, lf_h, lp_h, ll_h, bu_h, bd_h, u1_h, d1_h, u2_h, d2_h, ur_h, dr_h,
    out_ref,
    src, lf, lp, ll, bu, bd, u1, d1, u2, d2, ur, dr,
    sp, part, pre_leaf, pre_box, pre_mid,
    a_s, a_r, ai_s, ai_r,
    b_s, b_r, bi_r, si, b2_r,
    c1_s, c1_r, c2_s, c2_r, rs,
    d_s, d_r, d_all, e_s, e_r, e_all,
    load_sem, send_sem, recv_sem,
):
    gx = lax.axis_index("gx")
    gy = lax.axis_index("gy")
    x, core = gx // 2, gx % 2
    y, z = gy % 4, gy // 4
    zl, zh = z % 4, z // 4

    pairs = (
        (src_h, src), (lf_h, lf), (bu_h, bu), (u1_h, u1), (u2_h, u2), (lp_h, lp),
        (ur_h, ur), (bd_h, bd), (d1_h, d1), (d2_h, d2), (dr_h, dr), (ll_h, ll),
    )
    loads = [
        pltpu.make_async_copy(h, v, load_sem.at[i]) for i, (h, v) in enumerate(pairs)
    ]
    (l_src, l_lf, l_bu, l_u1, l_u2, l_lp, l_ur, l_bd, l_d1, l_d2, l_dr, l_ll) = loads
    for l in loads[:4]:
        l.start()

    def across(dx, dc, dy):
        return (((x + dx) % 4) * 2 + (core + dc) % 2, z * 4 + (y + dy) % 4)

    def in_plane(dz, dy):
        return (gx, (zh * 4 + (zl + dz) % 4) * 4 + (y + dy) % 4)

    def along_z(dz):
        return (gx, ((z + dz) % 8) * 4 + y)

    barrier = pltpu.get_barrier_semaphore()
    greet = []
    for dz in range(4):
        for dy in range(4):
            if dz or dy:
                greet.append(in_plane(dz, dy))
    for dx in range(4):
        for dc in range(2):
            for dy in range(4):
                if dx or dc:
                    greet.append(across(dx, dc, dy))
    for far in range(4):
        greet.append((gx, ((1 - zh) * 4 + far) * 4 + y))
    for device in greet:
        pl.semaphore_signal(barrier, inc=1, device_id=device, device_id_type=MESH)
    for l in loads[4:]:
        l.start()

    sends = []

    def send(s, d, stage, device):
        c = pltpu.make_async_remote_copy(
            src_ref=s,
            dst_ref=d,
            send_sem=send_sem.at[stage],
            recv_sem=recv_sem.at[stage],
            device_id=device,
            device_id_type=MESH,
        )
        c.start()

    def arrived(ref, stage):
        pltpu.make_async_copy(ref, ref, recv_sem.at[stage]).wait()

    def sent(ref, stage):
        pltpu.make_async_copy(ref, ref, send_sem.at[stage]).wait()

    l_src.wait()
    rows = lax.broadcasted_iota(jnp.int32, (256, 256), 0)
    cols = lax.broadcasted_iota(jnp.int32, (256, 256), 1)
    pick = ((rows % 16) * 16 + rows // 16 == cols).astype(F32).astype(BF)
    sp[...] = nn(pick, src[...].reshape(R * LEAF, 256)).astype(BF)
    l_lf.wait()
    lane = lax.broadcasted_iota(jnp.int32, (R, 128), 1)
    blocks = []
    for m in range(8):
        f = nt(sp[32 * m : 32 * m + 32, :], lf[128 * m : 128 * m + 128, :])
        blocks.append(jnp.where(lane < 64, f[:16], f[16:]).astype(BF))
    flux = jnp.concatenate(blocks, axis=1)
    l_bu.wait()
    box_flux = nt(flux, bu[384:, :]).astype(BF)
    l_u1.wait()
    first_flux = nn(box_flux, u1[:, 256:])
    for j in range(4):
        a_s[j] = first_flux[:, 128 * j : 128 * j + 128].astype(BF)
    pl.semaphore_wait(barrier, len(greet))
    for k in (2, 1, 3):
        send(a_s.at[(y + k) % 4], a_r.at[k - 1], ST_A, in_plane(0, k))
    first_if = nn(box_flux, u1[:, :256])
    ai_s[...] = first_if.astype(BF)
    for k in (2, 1, 3):
        send(ai_s, ai_r.at[k - 1], ST_AI, in_plane(0, k))
    box_if = nt(flux, bu[:384, :]).astype(BF)
    l_bd.wait()
    pre_leaf[...] = nt(box_if, bd[:, :384])
    l_u2.wait()

    arrived(a_r, ST_A)
    piece = a_s[y].astype(F32)
    for k in range(3):
        piece = piece + a_r[k].astype(F32)
    second_piece = piece.astype(BF)
    second_flux = nn(second_piece, u2[:, 512:])
    for j in range(8):
        b_s[4 + j] = second_flux[:, 128 * j : 128 * j + 128].astype(BF)
    plane = [(dz, dy) for dz in (2, 3, 1, 0) for dy in (2, 1, 3, 0) if dz or dy]
    for dz, dy in plane:
        to_z, to_y = (zl + dz) % 4, (y + dy) % 4
        send(
            b_s.at[4 + to_z * 2 + to_y // 2],
            b_r.at[dz * 4 + dy - 1],
            ST_B,
            in_plane(dz, dy),
        )
    second_if = nn(second_piece, u2[:, :512])
    for j in range(4):
        b_s[j] = second_if[:, 128 * j : 128 * j + 128].astype(BF)
    for dz, dy in plane:
        send(b_s.at[(zl + dz) % 4], bi_r.at[dz * 4 + dy - 1], ST_BI, in_plane(dz, dy))

    arrived(ai_r, ST_AI)
    whole = ai_s[...].astype(F32)
    for k in range(3):
        whole = whole + ai_r[k].astype(F32)
    l_d1.wait()
    pre_box[...] = nt(whole.astype(BF), d1[:, :256])
    l_lp.wait()
    for l in range(LEAF):
        part[l] = nn(sp[16 * l : 16 * l + 16, :], lp[256 * l : 256 * l + 256, :])
    l_ur.wait()

    arrived(b_r, ST_B)
    total = b_s[4 + zl * 2 + y // 2].astype(F32)
    for k in range(15):
        total = total + b_r[k].astype(F32)
    odd = jnp.broadcast_to(y % 2, (R, 64)) == 1
    root_piece = jnp.where(odd, total[:, 64:], total[:, :64]).astype(BF)
    for j in range(16):
        t = nn(root_piece, ur[:, 384 * j : 384 * j + 384])
        c1_s[0, j] = t[:8].astype(BF)
        c1_s[1, j] = t[8:].astype(BF)
    third = [
        (dx, dc, dy)
        for dx in (2, 1, 3, 0)
        for dy in (2, 1, 3, 0)
        for dc in (0, 1)
        if dx or dc or dy
    ]
    for dx, dc, dy in third:
        to = ((x + dx) % 4) * 4 + (y + dy) % 4
        send(
            c1_s.at[(core + dc) % 2, to],
            c1_r.at[(dx * 4 + dy) * 2 + dc - 1],
            ST_C1,
            across(dx, dc, dy),
        )
    arrived(bi_r, ST_BI)
    total = b_s[zl].astype(F32)
    for k in range(15):
        total = total + bi_r[k].astype(F32)
    si[zl] = total.astype(BF)
    for dz in (2, 1, 3):
        send(si.at[zl], si.at[zl], ST_B2, in_plane(dz, 0))
    l_d2.wait()
    l_dr.wait()
    l_ll.wait()

    arrived(c1_r, ST_C1)
    mine = c1_s[core, x * 4 + y].astype(F32)
    for k in range(31):
        mine = mine + c1_r[k].astype(F32)
    c2_s[...] = mine.astype(BF)
    for dz in (4, 3, 5, 2, 6, 1, 7):
        send(c2_s, c2_r.at[dz - 1], ST_C2, along_z(dz))
    arrived(b2_r, ST_B2)
    second_iface = jnp.concatenate([si[j] for j in range(4)], axis=1)
    pre_mid[...] = nt(second_iface, d2[:, :512])

    arrived(c2_r, ST_C2)
    for k in range(7):
        mine = mine + c2_r[k].astype(F32)
    rs[core, x * 4 + y] = mine.astype(BF)
    for dx, dc, dy in third:
        send(
            rs.at[core, x * 4 + y],
            rs.at[core, x * 4 + y],
            ST_C3,
            across(dx, dc, dy),
        )
    arrived(c1_r, ST_C3)
    top = jnp.zeros((R, 64), F32)
    for j in range(16):
        v = jnp.concatenate([rs[0, j].astype(F32), rs[1, j].astype(F32)], axis=0)
        top = top + nt(v.astype(BF), dr[:, 384 * j : 384 * j + 384])
    twice = jnp.concatenate([top, top], axis=1)
    half = jnp.broadcast_to(y % 2, (R, 128))
    here = zl * 4 + y
    d_all[here] = jnp.where(lane // 64 == half, twice, 0.0).astype(BF)
    for dz, dy in plane:
        send(d_all.at[here], d_all.at[here], ST_D, in_plane(dz, dy))
    arrived(b_r, ST_D)
    top_bound = jnp.concatenate(
        [d_all[2 * j] + d_all[2 * j + 1] for j in range(8)], axis=1
    )
    e_all[y] = (pre_mid[...] + nt(top_bound, d2[:, 512:])).astype(BF)
    for k in (2, 1, 3):
        send(e_all.at[y], e_all.at[y], ST_E, in_plane(0, k))
    arrived(a_r, ST_E)
    mid_bound = jnp.concatenate([e_all[j] for j in range(4)], axis=1)
    box_bound = (pre_box[...] + nt(mid_bound, d1[:, 256:])).astype(BF)
    leaf_bound = (pre_leaf[...] + nt(box_bound, bd[:, 384:])).astype(BF)
    low = lane < 64
    zero = jnp.zeros((R, 128), BF)
    for m in range(8):
        pair = leaf_bound[:, 128 * m : 128 * m + 128]
        both = jnp.concatenate(
            [jnp.where(low, pair, zero), jnp.where(low, zero, pair)], axis=0
        )
        lifted = nn(both, ll[128 * m : 128 * m + 128, :])
        out_ref[:, 2 * m, :] = lifted[:16] + part[2 * m]
        out_ref[:, 2 * m + 1, :] = lifted[16:] + part[2 * m + 1]

    sent(a_r, ST_A)
    sent(ai_r, ST_AI)
    sent(b_r, ST_B)
    sent(bi_r, ST_BI)
    sent(b2_r, ST_B2)
    sent(c1_r, ST_C1)
    sent(c2_r, ST_C2)
    sent(c1_r, ST_C3)
    sent(b_r, ST_D)
    sent(a_r, ST_E)


def per_device(*args):
    shapes = [a.shape for a in args]
    leaves = args[0].shape[1]
    return pl.pallas_call(
        kernel,
        out_shape=jax.ShapeDtypeStruct((R, leaves, 256), F32),
        in_specs=[pl.BlockSpec(memory_space=pl.ANY)] * 12,
        out_specs=pl.BlockSpec(memory_space=pltpu.VMEM),
        scratch_shapes=[pltpu.VMEM(s, BF) for s in shapes]
        + [
            pltpu.VMEM((256, 256), BF),
            pltpu.VMEM((16, 16, 256), F32),
            pltpu.VMEM((16, 1024), F32),
            pltpu.VMEM((16, 256), F32),
            pltpu.VMEM((16, 128), F32),
            pltpu.VMEM((4, 16, 128), BF),
            pltpu.VMEM((3, 16, 128), BF),
            pltpu.VMEM((16, 256), BF),
            pltpu.VMEM((3, 16, 256), BF),
            pltpu.VMEM((12, 16, 128), BF),
            pltpu.VMEM((15, 16, 128), BF),
            pltpu.VMEM((15, 16, 128), BF),
            pltpu.VMEM((4, 16, 128), BF),
            pltpu.VMEM((3, 16, 128), BF),
            pltpu.VMEM((2, 16, 8, 384), BF),
            pltpu.VMEM((31, 8, 384), BF),
            pltpu.VMEM((8, 384), BF),
            pltpu.VMEM((7, 8, 384), BF),
            pltpu.VMEM((2, 16, 8, 384), BF),
            pltpu.VMEM((16, 128), BF),
            pltpu.VMEM((15, 16, 128), BF),
            pltpu.VMEM((16, 16, 128), BF),
            pltpu.VMEM((16, 128), BF),
            pltpu.VMEM((3, 16, 128), BF),
            pltpu.VMEM((4, 16, 128), BF),
            pltpu.SemaphoreType.DMA((12,)),
            pltpu.SemaphoreType.DMA((N_STAGE,)),
            pltpu.SemaphoreType.DMA((N_STAGE,)),
        ],
        compiler_params=pltpu.CompilerParams(
            collective_id=0, has_side_effects=True, vmem_limit_bytes=60 * 1024 * 1024
        ),
    )(*args)


def solution(mesh):
    both = ("gx", "gy")
    return jax.shard_map(
        per_device,
        mesh=mesh,
        in_specs=(P(None, both, None),) + (P(both, None),) * 11,
        out_specs=P(None, both, None),
        check_vma=False,
    )
```

```python
import jax
import jax.numpy as jnp
from jax import lax
from jax.experimental import pallas as pl
from jax.experimental.pallas import tpu as pltpu
from jax.sharding import PartitionSpec as P

MESH = pl.DeviceIdType.MESH
BF = jnp.bfloat16
F32 = jnp.float32

R = 16
LEAF = 16
ST_A, ST_AI, ST_B, ST_BI, ST_B2, ST_C1, ST_C2, ST_C3, ST_D, ST_E = range(10)
N_STAGE = 10


def nt(x, w):
    return lax.dot_general(x, w, (((1,), (1,)), ((), ())), preferred_element_type=F32)


def nn(x, w):
    return jnp.dot(x, w, preferred_element_type=F32)


def kernel(
    src_h, lf_h, lp_h, bu_h, bd_h, u1_h, d1_h, u2_h, d2_h, ur_h, dr_h,
    lb_ref, part,
    src, lf, lp, bu, bd, u1, d1, u2, d2, ur, dr,
    sp, pre_leaf, pre_mid, joint,
    a_s, a_r, ai_s, ai_r,
    b_s, b_r, bi_s, bi_r, si, b2_r,
    c1_s, c1_r, c2_s, c2_r, rs,
    d_all, e_all,
    load_sem, send_sem, recv_sem,
):
    gx = lax.axis_index("gx")
    gy = lax.axis_index("gy")
    x, core = gx // 2, gx % 2
    y, z = gy % 4, gy // 4
    zl, zh = z % 4, z // 4

    pairs = (
        (src_h, src), (lf_h, lf), (bu_h.at[384:], bu.at[384:]), (u1_h, u1),
        (u2_h, u2), (ur_h, ur), (bu_h.at[:384], bu.at[:384]), (lp_h, lp),
        (bd_h, bd), (d1_h, d1), (d2_h, d2), (dr_h, dr),
    )
    loads = [
        pltpu.make_async_copy(h, v, load_sem.at[i]) for i, (h, v) in enumerate(pairs)
    ]
    (l_src, l_lf, l_bu, l_u1, l_u2, l_ur, l_bi, l_lp, l_bd, l_d1, l_d2, l_dr) = loads
    for l in loads[:4]:
        l.start()

    def across(dx, dc, dy):
        return (((x + dx) % 4) * 2 + (core + dc) % 2, z * 4 + (y + dy) % 4)

    def in_plane(dz, dy):
        return (gx, (zh * 4 + (zl + dz) % 4) * 4 + (y + dy) % 4)

    def along_z(dz):
        return (gx, ((z + dz) % 8) * 4 + y)

    barrier = pltpu.get_barrier_semaphore()
    greet = [(gx, ((1 - zh) * 4 + far) * 4 + y) for far in range(4)]
    plane = [(dz, dy) for dz in (2, 3, 1, 0) for dy in (2, 1, 3, 0) if dz or dy]
    third = [
        (dx, dc, dy)
        for dx in (2, 1, 3, 0)
        for dy in (2, 1, 3, 0)
        for dc in (0, 1)
        if dx or dc or dy
    ]
    greet += [in_plane(dz, dy) for dz, dy in plane]
    greet += [across(dx, dc, dy) for dx, dc, dy in third if dx or dc]
    for device in greet:
        pl.semaphore_signal(barrier, inc=1, device_id=device, device_id_type=MESH)

    def send(s, d, stage, device):
        c = pltpu.make_async_remote_copy(
            src_ref=s,
            dst_ref=d,
            send_sem=send_sem.at[stage],
            recv_sem=recv_sem.at[stage],
            device_id=device,
            device_id_type=MESH,
        )
        c.start()

    def arrived(ref, stage):
        pltpu.make_async_copy(ref, ref, recv_sem.at[stage]).wait()

    def sent(ref, stage):
        pltpu.make_async_copy(ref, ref, send_sem.at[stage]).wait()

    l_src.wait()
    rows = lax.broadcasted_iota(jnp.int32, (256, 256), 0)
    cols = lax.broadcasted_iota(jnp.int32, (256, 256), 1)
    pick = ((rows % 16) * 16 + rows // 16 == cols).astype(F32).astype(BF)
    sp[...] = nn(pick, src[...].reshape(R * LEAF, 256)).astype(BF)
    l_lf.wait()
    lane = lax.broadcasted_iota(jnp.int32, (R, 128), 1)
    low = lax.broadcasted_iota(jnp.int32, (8, 128), 1) < 64

    def pack(v):
        up, down = v[:8], v[8:]
        first = jnp.where(low, up, pltpu.roll(down, 64, 1))
        second = jnp.where(low, pltpu.roll(up, 64, 1), down)
        return first.astype(BF), second.astype(BF)

    def unpack(first, second):
        first, second = first.astype(F32), second.astype(F32)
        up = jnp.where(low, first, pltpu.roll(second, 64, 1))
        down = jnp.where(low, pltpu.roll(first, 64, 1), second)
        return jnp.concatenate([up, down], axis=0).astype(BF)

    blocks = []
    for m in range(8):
        f = nt(sp[32 * m : 32 * m + 32, :], lf[128 * m : 128 * m + 128, :])
        blocks.append(jnp.where(lane < 64, f[:16], f[16:]).astype(BF))
    flux = jnp.concatenate(blocks, axis=1)
    l_bu.wait()
    box_flux = nt(flux, bu[384:, :]).astype(BF)
    l_u1.wait()
    for l in loads[4:]:
        l.start()
    first_flux = nn(box_flux, u1[:, 256:])
    for j in range(4):
        a_s[j] = first_flux[:, 128 * j : 128 * j + 128].astype(BF)
    pl.semaphore_wait(barrier, len(greet))
    for k in (2, 1, 3):
        send(a_s.at[(y + k) % 4], a_r.at[k - 1], ST_A, in_plane(0, k))
    first_if = nn(box_flux, u1[:, :256])
    ai_s[...] = first_if.astype(BF)
    for k in (2, 1, 3):
        send(ai_s, ai_r.at[k - 1], ST_AI, in_plane(0, k))
    l_u2.wait()

    arrived(a_r, ST_A)
    piece = a_s[y].astype(F32)
    for k in range(3):
        piece = piece + a_r[k].astype(F32)
    second_piece = piece.astype(BF)
    second_flux = nn(second_piece, u2[:, 512:])
    for j in range(8):
        b_s[2 * j], b_s[2 * j + 1] = pack(second_flux[:, 128 * j : 128 * j + 128])
    for dz, dy in plane:
        to = (zl + dz) % 4 * 4 + (y + dy) % 4
        send(b_s.at[to], b_r.at[dz * 4 + dy - 1], ST_B, in_plane(dz, dy))
    second_if = nn(second_piece, u2[:, :512])
    for j in range(4):
        bi_s[2 * j], bi_s[2 * j + 1] = pack(second_if[:, 128 * j : 128 * j + 128])
    l_bi.wait()
    box_if = nt(flux, bu[:384, :]).astype(BF)
    l_ur.wait()

    arrived(b_r, ST_B)
    here = zl * 4 + y
    total = b_s[here].astype(F32)
    for k in range(15):
        total = total + b_r[k].astype(F32)
    root_piece = jnp.concatenate([total[:, :64], total[:, 64:]], axis=0).astype(BF)
    for j in range(16):
        t = nn(root_piece, ur[:, 384 * j : 384 * j + 384])
        c1_s[0, j] = t[:8].astype(BF)
        c1_s[1, j] = t[8:].astype(BF)
    for dx, dc, dy in third:
        to = ((x + dx) % 4) * 4 + (y + dy) % 4
        send(
            c1_s.at[(core + dc) % 2, to],
            c1_r.at[(dx * 4 + dy) * 2 + dc - 1],
            ST_C1,
            across(dx, dc, dy),
        )
    for dz, dy in plane:
        to = (zl + dz) % 2 * 4 + (y + dy) % 4
        send(bi_s.at[to], bi_r.at[dz * 4 + dy - 1], ST_BI, in_plane(dz, dy))
    l_lp.wait()
    for l in range(LEAF):
        part[l] = nn(sp[16 * l : 16 * l + 16, :], lp[256 * l : 256 * l + 256, :])
    arrived(ai_r, ST_AI)
    whole = ai_s[...].astype(F32)
    for k in range(3):
        whole = whole + ai_r[k].astype(F32)
    l_d1.wait()
    l_bd.wait()
    box_part = nt(whole.astype(BF), d1[:, :256]).astype(BF)
    pre_leaf[...] = nt(box_if, bd[:, :384]) + nt(box_part, bd[:, 384:])
    l_d2.wait()
    l_dr.wait()

    arrived(c1_r, ST_C1)
    mine = c1_s[core, x * 4 + y].astype(F32)
    for k in range(31):
        mine = mine + c1_r[k].astype(F32)
    c2_s[...] = mine.astype(BF)
    for dz in (4, 3, 5, 2, 6, 1, 7):
        send(c2_s, c2_r.at[dz - 1], ST_C2, along_z(dz))
    arrived(bi_r, ST_BI)
    own = zl % 2 * 4 + y
    total = bi_s[own].astype(F32)
    for k in range(15):
        total = total + bi_r[k].astype(F32)
    si[own] = total.astype(BF)
    flip = zl + 1 - zl % 2 * 2
    for dy in (2, 1, 3, 0):
        send(si.at[own], si.at[own], ST_B2, (gx, (zh * 4 + flip) * 4 + (y + dy) % 4))
    for dy in (2, 1, 3):
        send(si.at[own], si.at[own], ST_B2, in_plane(0, dy))

    arrived(c2_r, ST_C2)
    for k in range(7):
        mine = mine + c2_r[k].astype(F32)
    rs[core, x * 4 + y] = mine.astype(BF)
    for dx, dc, dy in third:
        send(
            rs.at[core, x * 4 + y],
            rs.at[core, x * 4 + y],
            ST_C3,
            across(dx, dc, dy),
        )
    for h in range(2):
        joint[:, 256 * h : 256 * h + 256] = nn(
            bd[:, 384:], d1[:, 256 + 256 * h : 512 + 256 * h]
        ).astype(BF)
    arrived(b2_r, ST_B2)
    second_iface = jnp.concatenate(
        [unpack(si[2 * j], si[2 * j + 1]) for j in range(4)], axis=1
    )
    pre_mid[...] = nt(second_iface, d2[:, :512])
    arrived(c1_r, ST_C3)
    top = jnp.zeros((R, 64), F32)
    for j in range(16):
        v = jnp.concatenate([rs[0, j].astype(F32), rs[1, j].astype(F32)], axis=0)
        top = top + nt(v.astype(BF), dr[:, 384 * j : 384 * j + 384])
    d_all[here] = jnp.concatenate([top[:8], top[8:]], axis=1).astype(BF)
    for dz, dy in plane:
        send(d_all.at[here], d_all.at[here], ST_D, in_plane(dz, dy))
    arrived(b_r, ST_D)
    top_bound = jnp.concatenate(
        [unpack(d_all[2 * j], d_all[2 * j + 1]) for j in range(8)], axis=1
    )
    e_all[y] = (pre_mid[...] + nt(top_bound, d2[:, 512:])).astype(BF)
    for k in (2, 1, 3):
        send(e_all.at[y], e_all.at[y], ST_E, in_plane(0, k))
    arrived(a_r, ST_E)
    mid_bound = jnp.concatenate([e_all[j] for j in range(4)], axis=1)
    lb_ref[...] = (pre_leaf[...] + nt(mid_bound, joint[...])).astype(BF)

    sent(a_r, ST_A)
    sent(ai_r, ST_AI)
    sent(b_r, ST_B)
    sent(bi_r, ST_BI)
    sent(b2_r, ST_B2)
    sent(c1_r, ST_C1)
    sent(c2_r, ST_C2)
    sent(c1_r, ST_C3)
    sent(b_r, ST_D)
    sent(a_r, ST_E)


def lift(lb_ref, part_ref, ll_ref, out_ref):
    low = lax.broadcasted_iota(jnp.int32, (R, 128), 1) < 64
    zero = jnp.zeros((R, 128), BF)
    for m in range(8):
        pair = lb_ref[:, 128 * m : 128 * m + 128]
        both = jnp.concatenate(
            [jnp.where(low, pair, zero), jnp.where(low, zero, pair)], axis=0
        )
        lifted = nn(both, ll_ref[128 * m : 128 * m + 128, :])
        out_ref[:, 2 * m, :] = lifted[:16] + part_ref[2 * m]
        out_ref[:, 2 * m + 1, :] = lifted[16:] + part_ref[2 * m + 1]


def per_device(src, lf, lp, ll, bu, bd, u1, d1, u2, d2, ur, dr):
    args = (src, lf, lp, bu, bd, u1, d1, u2, d2, ur, dr)
    vmem = pl.BlockSpec(memory_space=pltpu.VMEM)
    lb, part = pl.pallas_call(
        kernel,
        out_shape=(
            jax.ShapeDtypeStruct((R, 1024), BF),
            jax.ShapeDtypeStruct((LEAF, R, 256), F32),
        ),
        in_specs=[pl.BlockSpec(memory_space=pltpu.HBM)] * 11,
        out_specs=(vmem, vmem),
        scratch_shapes=[pltpu.VMEM(a.shape, BF) for a in args]
        + [
            pltpu.VMEM((256, 256), BF),
            pltpu.VMEM((16, 1024), F32),
            pltpu.VMEM((16, 128), F32),
            pltpu.VMEM((1024, 512), BF),
            pltpu.VMEM((4, 16, 128), BF),
            pltpu.VMEM((3, 16, 128), BF),
            pltpu.VMEM((16, 256), BF),
            pltpu.VMEM((3, 16, 256), BF),
            pltpu.VMEM((16, 8, 128), BF),
            pltpu.VMEM((15, 8, 128), BF),
            pltpu.VMEM((8, 8, 128), BF),
            pltpu.VMEM((15, 8, 128), BF),
            pltpu.VMEM((8, 8, 128), BF),
            pltpu.VMEM((7, 8, 128), BF),
            pltpu.VMEM((2, 16, 8, 384), BF),
            pltpu.VMEM((31, 8, 384), BF),
            pltpu.VMEM((8, 384), BF),
            pltpu.VMEM((7, 8, 384), BF),
            pltpu.VMEM((2, 16, 8, 384), BF),
            pltpu.VMEM((16, 8, 128), BF),
            pltpu.VMEM((4, 16, 128), BF),
            pltpu.SemaphoreType.DMA((12,)),
            pltpu.SemaphoreType.DMA((N_STAGE,)),
            pltpu.SemaphoreType.DMA((N_STAGE,)),
        ],
        compiler_params=pltpu.CompilerParams(
            collective_id=0, has_side_effects=True, vmem_limit_bytes=32 * 1024 * 1024
        ),
    )(*[pltpu.with_memory_space_constraint(a, pltpu.HBM) for a in args])
    return pl.pallas_call(
        lift,
        out_shape=jax.ShapeDtypeStruct((R, LEAF, 256), F32),
        in_specs=[vmem] * 3,
        out_specs=vmem,
        compiler_params=pltpu.CompilerParams(vmem_limit_bytes=8 * 1024 * 1024),
    )(lb, part, ll)


def solution(mesh):
    both = ("gx", "gy")
    return jax.shard_map(
        per_device,
        mesh=mesh,
        in_specs=(P(None, both, None),) + (P(both, None),) * 11,
        out_specs=P(None, both, None),
        check_vma=False,
    )
```

```python
import jax
import jax.numpy as jnp
from jax import lax
from jax.experimental import pallas as pl
from jax.experimental.pallas import tpu as pltpu
from jax.sharding import PartitionSpec as P

MESH = pl.DeviceIdType.MESH
BF = jnp.bfloat16
F32 = jnp.float32

R = 16
LEAF = 16
ST_A, ST_AI, ST_B, ST_BI, ST_B2, ST_C1, ST_C2, ST_D, ST_E = range(9)
ST_X, ST_C3, ST_F = 9, 13, 17
N_STAGE = 21


def nt(x, w):
    return lax.dot_general(x, w, (((1,), (1,)), ((), ())), preferred_element_type=F32)


def nn(x, w):
    return jnp.dot(x, w, preferred_element_type=F32)


def kernel(
    src_h, lf_h, lp_h, bu_h, bd_h, u1_h, d1_h, u2_h, d2_h, ur_h, dr_h,
    lb_ref, part,
    src, lf, lp, bu, bd, u1, d1, u2, d2, ur, dr,
    sp, pre_leaf, pre_mid, joint,
    a_s, a_r, ai_s, ai_r,
    b_s, b_r, bi_s, bi_r, si, b2_r,
    c1_s, c1_x, c1_t, c1_r, c2_s, c2_r, rs,
    d_all, e_all,
    load_sem, send_sem, recv_sem, round_sem,
):
    gx = lax.axis_index("gx")
    gy = lax.axis_index("gy")
    x, core = gx // 2, gx % 2
    y, z = gy % 4, gy // 4
    zl, zh = z % 4, z // 4

    pairs = (
        (src_h, src), (lf_h, lf), (bu_h.at[384:], bu.at[384:]), (u1_h, u1),
        (u2_h, u2), (ur_h, ur), (bu_h.at[:384], bu.at[:384]), (lp_h, lp),
        (bd_h, bd), (d1_h, d1), (d2_h, d2), (dr_h, dr),
    )
    loads = [
        pltpu.make_async_copy(h, v, load_sem.at[i]) for i, (h, v) in enumerate(pairs)
    ]
    (l_src, l_lf, l_bu, l_u1, l_u2, l_ur, l_bi, l_lp, l_bd, l_d1, l_d2, l_dr) = loads
    for l in loads[:4]:
        l.start()

    sibling = (x * 2 + 1 - core, gy)

    def across(dx, dy):
        return ((x + dx) % 4 * 2 + core, z * 4 + (y + dy) % 4)

    def in_plane(dz, dy):
        return (gx, (zh * 4 + (zl + dz) % 4) * 4 + (y + dy) % 4)

    def along_z(dz):
        return (gx, ((z + dz) % 8) * 4 + y)

    x_near = [across(1, 0), across(3, 0)]
    z_near = [along_z(1), along_z(7)]
    greet = [in_plane(0, 2), in_plane(0, 1), in_plane(0, 3), sibling] + z_near + x_near
    rounds = (z_near, z_near + x_near, z_near + x_near)
    barrier = pltpu.get_barrier_semaphore()
    for device in greet:
        pl.semaphore_signal(barrier, inc=1, device_id=device, device_id_type=MESH)

    def pass_on(n):
        if n == 0:
            pl.semaphore_wait(barrier, len(greet))
        else:
            pl.semaphore_wait(round_sem.at[n - 1], len(rounds[n - 1]))
        if n < 3:
            for device in rounds[n]:
                pl.semaphore_signal(
                    round_sem.at[n], inc=1, device_id=device, device_id_type=MESH
                )

    plane = [(dz, dy) for dz in (2, 3, 1, 0) for dy in (2, 1, 3, 0) if dz or dy]

    def send(s, d, stage, device):
        c = pltpu.make_async_remote_copy(
            src_ref=s,
            dst_ref=d,
            send_sem=send_sem.at[stage],
            recv_sem=recv_sem.at[stage],
            device_id=device,
            device_id_type=MESH,
        )
        c.start()

    def arrived(ref, stage):
        pltpu.make_async_copy(ref, ref, recv_sem.at[stage]).wait()

    def sent(ref, stage):
        pltpu.make_async_copy(ref, ref, send_sem.at[stage]).wait()

    l_src.wait()
    rows = lax.broadcasted_iota(jnp.int32, (256, 256), 0)
    cols = lax.broadcasted_iota(jnp.int32, (256, 256), 1)
    pick = ((rows % 16) * 16 + rows // 16 == cols).astype(F32).astype(BF)
    sp[...] = nn(pick, src[...].reshape(R * LEAF, 256)).astype(BF)
    l_lf.wait()
    lane = lax.broadcasted_iota(jnp.int32, (R, 128), 1)
    low = lax.broadcasted_iota(jnp.int32, (8, 128), 1) < 64

    def pack(v):
        up, down = v[:8], v[8:]
        first = jnp.where(low, up, pltpu.roll(down, 64, 1))
        second = jnp.where(low, pltpu.roll(up, 64, 1), down)
        return first.astype(BF), second.astype(BF)

    def unpack(first, second):
        first, second = first.astype(F32), second.astype(F32)
        up = jnp.where(low, first, pltpu.roll(second, 64, 1))
        down = jnp.where(low, pltpu.roll(first, 64, 1), second)
        return jnp.concatenate([up, down], axis=0).astype(BF)

    blocks = []
    for m in range(8):
        f = nt(sp[32 * m : 32 * m + 32, :], lf[128 * m : 128 * m + 128, :])
        blocks.append(jnp.where(lane < 64, f[:16], f[16:]).astype(BF))
    flux = jnp.concatenate(blocks, axis=1)
    pass_on(0)
    l_bu.wait()
    box_flux = nt(flux, bu[384:, :]).astype(BF)
    l_u1.wait()
    for l in loads[4:]:
        l.start()
    first_flux = nn(box_flux, u1[:, 256:])
    for j in range(4):
        a_s[j] = first_flux[:, 128 * j : 128 * j + 128].astype(BF)
    for k in (2, 1, 3):
        send(a_s.at[(y + k) % 4], a_r.at[k - 1], ST_A, in_plane(0, k))
    pass_on(1)
    first_if = nn(box_flux, u1[:, :256])
    ai_s[...] = first_if.astype(BF)
    for k in (2, 1, 3):
        send(ai_s, ai_r.at[k - 1], ST_AI, in_plane(0, k))
    pass_on(2)
    l_u2.wait()

    arrived(a_r, ST_A)
    piece = a_s[y].astype(F32)
    for k in range(3):
        piece = piece + a_r[k].astype(F32)
    second_piece = piece.astype(BF)
    second_flux = nn(second_piece, u2[:, 512:])
    for j in range(8):
        b_s[2 * j], b_s[2 * j + 1] = pack(second_flux[:, 128 * j : 128 * j + 128])
    pass_on(3)
    for dz, dy in plane:
        to = (zl + dz) % 4 * 4 + (y + dy) % 4
        send(b_s.at[to], b_r.at[dz * 4 + dy - 1], ST_B, in_plane(dz, dy))
    second_if = nn(second_piece, u2[:, :512])
    for j in range(4):
        bi_s[2 * j], bi_s[2 * j + 1] = pack(second_if[:, 128 * j : 128 * j + 128])
    l_bi.wait()
    box_if = nt(flux, bu[:384, :]).astype(BF)
    l_ur.wait()

    arrived(b_r, ST_B)
    here = zl * 4 + y
    total = b_s[here].astype(F32)
    for k in range(15):
        total = total + b_r[k].astype(F32)
    root_piece = jnp.concatenate([total[:, :64], total[:, 64:]], axis=0).astype(BF)
    reach = (2, 1, 3, 0)
    for n, dx in enumerate(reach):
        g = (x + dx) % 4
        t = nn(root_piece, ur[:, pl.ds(pl.multiple_of(1536 * g, 128), 1536)])
        for q in range(4):
            c1_s[0, 4 * g + q] = t[:8, 384 * q : 384 * q + 384].astype(BF)
            c1_s[1, 4 * g + q] = t[8:, 384 * q : 384 * q + 384].astype(BF)
        send(
            c1_s.at[1 - core, pl.ds(4 * g, 4)],
            c1_x.at[pl.ds(4 * g, 4)],
            ST_X + n,
            sibling,
        )
    for n, dx in enumerate(reach):
        g = (x + dx) % 4
        arrived(c1_r.at[:4], ST_X + n)
        for q in range(4):
            c1_t[4 * g + q] = (
                c1_s[core, 4 * g + q].astype(F32) + c1_x[4 * g + q].astype(F32)
            ).astype(BF)
        for dy in (2, 1, 3, 0):
            if dx or dy:
                send(
                    c1_t.at[4 * g + (y + dy) % 4],
                    c1_r.at[dx * 4 + dy - 1],
                    ST_C1,
                    across(dx, dy),
                )
    for dz, dy in plane:
        to = (zl + dz) % 2 * 4 + (y + dy) % 4
        send(bi_s.at[to], bi_r.at[dz * 4 + dy - 1], ST_BI, in_plane(dz, dy))
    l_lp.wait()
    for l in range(LEAF):
        part[l] = nn(sp[16 * l : 16 * l + 16, :], lp[256 * l : 256 * l + 256, :])
    arrived(ai_r, ST_AI)
    whole = ai_s[...].astype(F32)
    for k in range(3):
        whole = whole + ai_r[k].astype(F32)
    l_d1.wait()
    l_bd.wait()
    box_part = nt(whole.astype(BF), d1[:, :256]).astype(BF)
    pre_leaf[...] = nt(box_if, bd[:, :384]) + nt(box_part, bd[:, 384:])
    l_d2.wait()
    l_dr.wait()

    arrived(c1_r, ST_C1)
    corner = x * 4 + y
    mine = c1_s[core, corner].astype(F32) + c1_x[corner].astype(F32)
    for k in range(15):
        mine = mine + c1_r[k].astype(F32)
    c2_s[...] = mine.astype(BF)
    for dz in (4, 3, 5, 2, 6, 1, 7):
        send(c2_s, c2_r.at[dz - 1], ST_C2, along_z(dz))
    arrived(bi_r, ST_BI)
    own = zl % 2 * 4 + y
    total = bi_s[own].astype(F32)
    for k in range(15):
        total = total + bi_r[k].astype(F32)
    si[own] = total.astype(BF)
    flip = zl + 1 - zl % 2 * 2
    for dy in (2, 1, 3, 0):
        send(si.at[own], si.at[own], ST_B2, (gx, (zh * 4 + flip) * 4 + (y + dy) % 4))
    for dy in (2, 1, 3):
        send(si.at[own], si.at[own], ST_B2, in_plane(0, dy))

    arrived(c2_r, ST_C2)
    for k in range(7):
        mine = mine + c2_r[k].astype(F32)
    rs[core, corner] = mine.astype(BF)
    for n, dx in enumerate(reach):
        for dy in (2, 1, 3, 0):
            if dx or dy:
                send(rs.at[core, corner], rs.at[core, corner], ST_C3 + n, across(dx, dy))
    for h in range(2):
        joint[:, 256 * h : 256 * h + 256] = nn(
            bd[:, 384:], d1[:, 256 + 256 * h : 512 + 256 * h]
        ).astype(BF)
    arrived(b2_r, ST_B2)
    second_iface = jnp.concatenate(
        [unpack(si[2 * j], si[2 * j + 1]) for j in range(4)], axis=1
    )
    pre_mid[...] = nt(second_iface, d2[:, :512])
    top = jnp.zeros((R, 64), F32)
    for n in (3, 1, 2, 0):
        g = (x + 4 - reach[n]) % 4
        arrived(c1_r.at[: 4 if n < 3 else 3], ST_C3 + n)
        send(rs.at[core, pl.ds(4 * g, 4)], rs.at[core, pl.ds(4 * g, 4)], ST_F + n, sibling)
    for n in (3, 1, 2, 0):
        g = (x + 4 - reach[n]) % 4
        arrived(c1_r.at[:4], ST_F + n)
        v = jnp.concatenate(
            [
                jnp.concatenate(
                    [rs[0, 4 * g + q].astype(F32), rs[1, 4 * g + q].astype(F32)], axis=0
                ).astype(BF)
                for q in range(4)
            ],
            axis=1,
        )
        top = top + nt(v, dr[:, pl.ds(pl.multiple_of(1536 * g, 128), 1536)])
    d_all[here] = jnp.concatenate([top[:8], top[8:]], axis=1).astype(BF)
    for dz, dy in plane:
        send(d_all.at[here], d_all.at[here], ST_D, in_plane(dz, dy))
    arrived(b_r, ST_D)
    top_bound = jnp.concatenate(
        [unpack(d_all[2 * j], d_all[2 * j + 1]) for j in range(8)], axis=1
    )
    e_all[y] = (pre_mid[...] + nt(top_bound, d2[:, 512:])).astype(BF)
    for k in (2, 1, 3):
        send(e_all.at[y], e_all.at[y], ST_E, in_plane(0, k))
    arrived(a_r, ST_E)
    mid_bound = jnp.concatenate([e_all[j] for j in range(4)], axis=1)
    lb_ref[...] = (pre_leaf[...] + nt(mid_bound, joint[...])).astype(BF)

    sent(a_r, ST_A)
    sent(ai_r, ST_AI)
    sent(b_r, ST_B)
    sent(bi_r, ST_BI)
    sent(b2_r, ST_B2)
    sent(c1_r, ST_C1)
    sent(c2_r, ST_C2)
    for n in range(4):
        sent(c1_r.at[:4], ST_X + n)
        sent(c1_r.at[: 4 if n < 3 else 3], ST_C3 + n)
        sent(c1_r.at[:4], ST_F + n)
    sent(b_r, ST_D)
    sent(a_r, ST_E)


def lift(lb_ref, part_ref, ll_ref, out_ref):
    low = lax.broadcasted_iota(jnp.int32, (R, 128), 1) < 64
    zero = jnp.zeros((R, 128), BF)
    for m in range(8):
        pair = lb_ref[:, 128 * m : 128 * m + 128]
        both = jnp.concatenate(
            [jnp.where(low, pair, zero), jnp.where(low, zero, pair)], axis=0
        )
        lifted = nn(both, ll_ref[128 * m : 128 * m + 128, :])
        out_ref[:, 2 * m, :] = lifted[:16] + part_ref[2 * m]
        out_ref[:, 2 * m + 1, :] = lifted[16:] + part_ref[2 * m + 1]


def per_device(src, lf, lp, ll, bu, bd, u1, d1, u2, d2, ur, dr):
    args = (src, lf, lp, bu, bd, u1, d1, u2, d2, ur, dr)
    vmem = pl.BlockSpec(memory_space=pltpu.VMEM)
    lb, part = pl.pallas_call(
        kernel,
        out_shape=(
            jax.ShapeDtypeStruct((R, 1024), BF),
            jax.ShapeDtypeStruct((LEAF, R, 256), F32),
        ),
        in_specs=[pl.BlockSpec(memory_space=pltpu.HBM)] * 11,
        out_specs=(vmem, vmem),
        scratch_shapes=[pltpu.VMEM(a.shape, BF) for a in args]
        + [
            pltpu.VMEM((256, 256), BF),
            pltpu.VMEM((16, 1024), F32),
            pltpu.VMEM((16, 128), F32),
            pltpu.VMEM((1024, 512), BF),
            pltpu.VMEM((4, 16, 128), BF),
            pltpu.VMEM((3, 16, 128), BF),
            pltpu.VMEM((16, 256), BF),
            pltpu.VMEM((3, 16, 256), BF),
            pltpu.VMEM((16, 8, 128), BF),
            pltpu.VMEM((15, 8, 128), BF),
            pltpu.VMEM((8, 8, 128), BF),
            pltpu.VMEM((15, 8, 128), BF),
            pltpu.VMEM((8, 8, 128), BF),
            pltpu.VMEM((7, 8, 128), BF),
            pltpu.VMEM((2, 16, 8, 384), BF),
            pltpu.VMEM((16, 8, 384), BF),
            pltpu.VMEM((16, 8, 384), BF),
            pltpu.VMEM((15, 8, 384), BF),
            pltpu.VMEM((8, 384), BF),
            pltpu.VMEM((7, 8, 384), BF),
            pltpu.VMEM((2, 16, 8, 384), BF),
            pltpu.VMEM((16, 8, 128), BF),
            pltpu.VMEM((4, 16, 128), BF),
            pltpu.SemaphoreType.DMA((12,)),
            pltpu.SemaphoreType.DMA((N_STAGE,)),
            pltpu.SemaphoreType.DMA((N_STAGE,)),
            pltpu.SemaphoreType.REGULAR((3,)),
        ],
        compiler_params=pltpu.CompilerParams(
            collective_id=0, has_side_effects=True, vmem_limit_bytes=32 * 1024 * 1024
        ),
    )(*[pltpu.with_memory_space_constraint(a, pltpu.HBM) for a in args])
    return pl.pallas_call(
        lift,
        out_shape=jax.ShapeDtypeStruct((R, LEAF, 256), F32),
        in_specs=[vmem] * 3,
        out_specs=vmem,
        compiler_params=pltpu.CompilerParams(vmem_limit_bytes=8 * 1024 * 1024),
    )(lb, part, ll)


def solution(mesh):
    both = ("gx", "gy")
    return jax.shard_map(
        per_device,
        mesh=mesh,
        in_specs=(P(None, both, None),) + (P(both, None),) * 11,
        out_specs=P(None, both, None),
        check_vma=False,
    )
```

```python
import jax
import jax.numpy as jnp
from jax import lax
from jax.experimental import pallas as pl
from jax.experimental.pallas import tpu as pltpu
from jax.sharding import PartitionSpec as P

MESH = pl.DeviceIdType.MESH
BF = jnp.bfloat16
F32 = jnp.float32

R = 16
LEAF = 16
ST_A, ST_AI, ST_B, ST_BI, ST_B2, ST_C1, ST_C2, ST_D, ST_E, ST_UR, ST_DR = range(11)
ST_C3 = 11
N_STAGE = 15


def nt(x, w):
    return lax.dot_general(x, w, (((1,), (1,)), ((), ())), preferred_element_type=F32)


def nn(x, w):
    return jnp.dot(x, w, preferred_element_type=F32)


def kernel(
    src_h, lf_h, lp_h, bu_h, bd_h, u1_h, d1_h, u2_h, d2_h, ur_h, dr_h,
    lb_ref, part,
    src, lf, lp, bu, bd, u1, d1, u2, d2, ur, dr,
    sp, pre_leaf, pre_mid, joint,
    a_s, a_r, ai_s, ai_r,
    b_s, b_r, bi_s, bi_r, si, b2_r,
    c1_s, c1_r, c2_s, c2_r, rs,
    d_s, d_all, e_all,
    load_sem, send_sem, recv_sem, round_sem,
):
    gx = lax.axis_index("gx")
    gy = lax.axis_index("gy")
    x, core = gx // 2, gx % 2
    y, z = gy % 4, gy // 4
    zl, zh = z % 4, z // 4

    pairs = (
        (src_h, src), (lf_h, lf), (bu_h.at[384:], bu.at[384:]), (u1_h, u1),
        (u2_h, u2), (ur_h, ur.at[:64]), (bu_h.at[:384], bu.at[:384]), (lp_h, lp),
        (bd_h, bd), (d1_h, d1), (d2_h, d2), (dr_h, dr.at[:64]),
    )
    loads = [
        pltpu.make_async_copy(h, v, load_sem.at[i]) for i, (h, v) in enumerate(pairs)
    ]
    (l_src, l_lf, l_bu, l_u1, l_u2, l_ur, l_bi, l_lp, l_bd, l_d1, l_d2, l_dr) = loads
    for l in loads[:4]:
        l.start()

    sibling = (x * 2 + 1 - core, gy)

    def across(dx, dy):
        return ((x + dx) % 4 * 2 + core, z * 4 + (y + dy) % 4)

    def in_plane(dz, dy):
        return (gx, (zh * 4 + (zl + dz) % 4) * 4 + (y + dy) % 4)

    def beside(dz, dy):
        return (sibling[0], (zh * 4 + (zl + dz) % 4) * 4 + (y + dy) % 4)

    def along_z(dz):
        return (gx, ((z + dz) % 8) * 4 + y)

    x_near = [across(1, 0), across(3, 0)]
    z_near = [along_z(1), along_z(7)]
    greet = [in_plane(0, k) for k in (2, 1, 3)] + [beside(0, k) for k in (2, 1, 3, 0)]
    greet += z_near + x_near
    rounds = (z_near, z_near + x_near, z_near + x_near)
    barrier = pltpu.get_barrier_semaphore()
    for device in greet:
        pl.semaphore_signal(barrier, inc=1, device_id=device, device_id_type=MESH)

    def pass_on(n):
        if n == 0:
            pl.semaphore_wait(barrier, len(greet))
        else:
            pl.semaphore_wait(round_sem.at[n - 1], len(rounds[n - 1]))
        if n < 3:
            for device in rounds[n]:
                pl.semaphore_signal(
                    round_sem.at[n], inc=1, device_id=device, device_id_type=MESH
                )

    plane = [(dz, dy) for dz in (2, 3, 1, 0) for dy in (2, 1, 3, 0) if dz or dy]

    def send(s, d, stage, device):
        c = pltpu.make_async_remote_copy(
            src_ref=s,
            dst_ref=d,
            send_sem=send_sem.at[stage],
            recv_sem=recv_sem.at[stage],
            device_id=device,
            device_id_type=MESH,
        )
        c.start()

    def arrived(ref, stage):
        pltpu.make_async_copy(ref, ref, recv_sem.at[stage]).wait()

    def sent(ref, stage):
        pltpu.make_async_copy(ref, ref, send_sem.at[stage]).wait()

    l_src.wait()
    rows = lax.broadcasted_iota(jnp.int32, (256, 256), 0)
    cols = lax.broadcasted_iota(jnp.int32, (256, 256), 1)
    pick = ((rows % 16) * 16 + rows // 16 == cols).astype(F32).astype(BF)
    sp[...] = nn(pick, src[...].reshape(R * LEAF, 256)).astype(BF)
    quarter = lax.broadcasted_iota(jnp.int32, (8, 128), 0) < 4
    keep = quarter == (lax.broadcasted_iota(jnp.int32, (8, 128), 1) < 64)

    def swap(v):
        return jnp.where(keep, v, pltpu.roll(pltpu.roll(v, 64, 1), 4, 0))

    l_lf.wait()
    lane = lax.broadcasted_iota(jnp.int32, (R, 128), 1)
    low = lax.broadcasted_iota(jnp.int32, (8, 128), 1) < 64

    def pack(v):
        up, down = v[:8], v[8:]
        first = jnp.where(low, up, pltpu.roll(down, 64, 1))
        second = jnp.where(low, pltpu.roll(up, 64, 1), down)
        return first.astype(BF), second.astype(BF)

    def unpack(first, second):
        first, second = first.astype(F32), second.astype(F32)
        up = jnp.where(low, first, pltpu.roll(second, 64, 1))
        down = jnp.where(low, pltpu.roll(first, 64, 1), second)
        return jnp.concatenate([up, down], axis=0).astype(BF)

    blocks = []
    for m in range(8):
        f = nt(sp[32 * m : 32 * m + 32, :], lf[128 * m : 128 * m + 128, :])
        blocks.append(jnp.where(lane < 64, f[:16], f[16:]).astype(BF))
    flux = jnp.concatenate(blocks, axis=1)
    pass_on(0)
    send(ur_h, ur.at[64:], ST_UR, sibling)
    send(dr_h, dr.at[64:], ST_DR, sibling)
    l_bu.wait()
    box_flux = nt(flux, bu[384:, :]).astype(BF)
    l_u1.wait()
    for l in loads[4:]:
        l.start()
    first_flux = nn(box_flux, u1[:, 256:])
    for j in range(4):
        a_s[j] = first_flux[:, 128 * j : 128 * j + 128].astype(BF)
    for k in (2, 1, 3):
        send(a_s.at[(y + k) % 4], a_r.at[k - 1], ST_A, in_plane(0, k))
    pass_on(1)
    first_if = nn(box_flux, u1[:, :256])
    ai_s[...] = first_if.astype(BF)
    for k in (2, 1, 3):
        send(ai_s, ai_r.at[k - 1], ST_AI, in_plane(0, k))
    pass_on(2)
    l_u2.wait()

    arrived(a_r, ST_A)
    piece = a_s[y].astype(F32)
    for k in range(3):
        piece = piece + a_r[k].astype(F32)
    second_piece = piece.astype(BF)
    second_flux = nn(second_piece, u2[:, 512:])
    for j in range(8):
        for h in range(2):
            v = swap(second_flux[8 * h : 8 * h + 8, 128 * j : 128 * j + 128])
            b_s[h, 2 * j] = v[:4].astype(BF)
            b_s[h, 2 * j + 1] = v[4:].astype(BF)
    pass_on(3)
    for dz, dy in plane + [(0, 0)]:
        to = (zl + dz) % 4 * 4 + (y + dy) % 4
        slot = dz * 4 + dy - 1
        if dz or dy:
            send(b_s.at[core, to], b_r.at[slot], ST_B, in_plane(dz, dy))
        send(b_s.at[1 - core, to], b_r.at[16 + slot], ST_B, beside(dz, dy))
    second_if = nn(second_piece, u2[:, :512])
    for j in range(4):
        bi_s[2 * j], bi_s[2 * j + 1] = pack(second_if[:, 128 * j : 128 * j + 128])
    l_bi.wait()
    box_if = nt(flux, bu[:384, :]).astype(BF)
    l_ur.wait()

    arrived(b_r, ST_B)
    here = zl * 4 + y
    total = b_s[core, here].astype(F32)
    for k in range(15):
        total = total + b_r[k].astype(F32)
    other = b_r[15].astype(F32)
    for k in range(16, 31):
        other = other + b_r[k].astype(F32)
    root_piece = swap(jnp.concatenate([total, other], axis=0)).astype(BF)
    arrived(ur.at[64:], ST_UR)
    for j in range(16):
        c1_s[j] = nn(root_piece, ur[:, 384 * j : 384 * j + 384]).astype(BF)
    reach = (2, 1, 3, 0)
    for dx in reach:
        for dy in reach:
            if dx or dy:
                send(
                    c1_s.at[(x + dx) % 4 * 4 + (y + dy) % 4],
                    c1_r.at[dx * 4 + dy - 1],
                    ST_C1,
                    across(dx, dy),
                )
    for dz, dy in plane:
        to = (zl + dz) % 2 * 4 + (y + dy) % 4
        send(bi_s.at[to], bi_r.at[dz * 4 + dy - 1], ST_BI, in_plane(dz, dy))
    l_lp.wait()
    for l in range(LEAF):
        part[l] = nn(sp[16 * l : 16 * l + 16, :], lp[256 * l : 256 * l + 256, :])
    arrived(ai_r, ST_AI)
    whole = ai_s[...].astype(F32)
    for k in range(3):
        whole = whole + ai_r[k].astype(F32)
    l_d1.wait()
    l_bd.wait()
    box_part = nt(whole.astype(BF), d1[:, :256]).astype(BF)
    pre_leaf[...] = nt(box_if, bd[:, :384]) + nt(box_part, bd[:, 384:])
    l_d2.wait()
    l_dr.wait()

    arrived(c1_r, ST_C1)
    corner = x * 4 + y
    mine = c1_s[corner].astype(F32)
    for k in range(15):
        mine = mine + c1_r[k].astype(F32)
    c2_s[...] = mine.astype(BF)
    for dz in (4, 3, 5, 2, 6, 1, 7):
        send(c2_s, c2_r.at[dz - 1], ST_C2, along_z(dz))
    arrived(bi_r, ST_BI)
    own = zl % 2 * 4 + y
    total = bi_s[own].astype(F32)
    for k in range(15):
        total = total + bi_r[k].astype(F32)
    si[own] = total.astype(BF)
    flip = zl + 1 - zl % 2 * 2
    for dy in (2, 1, 3, 0):
        send(si.at[own], si.at[own], ST_B2, (gx, (zh * 4 + flip) * 4 + (y + dy) % 4))
    for dy in (2, 1, 3):
        send(si.at[own], si.at[own], ST_B2, in_plane(0, dy))

    arrived(c2_r, ST_C2)
    for k in range(7):
        mine = mine + c2_r[k].astype(F32)
    rs[corner] = mine.astype(BF)
    for n, dx in enumerate(reach):
        for dy in (2, 1, 3, 0):
            if dx or dy:
                send(rs.at[corner], rs.at[corner], ST_C3 + n, across(dx, dy))
    for h in range(2):
        joint[:, 256 * h : 256 * h + 256] = nn(
            bd[:, 384:], d1[:, 256 + 256 * h : 512 + 256 * h]
        ).astype(BF)
    arrived(b2_r, ST_B2)
    second_iface = jnp.concatenate(
        [unpack(si[2 * j], si[2 * j + 1]) for j in range(4)], axis=1
    )
    pre_mid[...] = nt(second_iface, d2[:, :512])
    arrived(dr.at[64:], ST_DR)
    top = jnp.zeros((8, 128), F32)
    for n in (3, 1, 2, 0):
        g = (x + 4 - reach[n]) % 4
        arrived(c1_r.at[: 4 if n < 3 else 3], ST_C3 + n)
        v = jnp.concatenate([rs[4 * g + q] for q in range(4)], axis=1)
        top = top + nt(v, dr[:, pl.ds(pl.multiple_of(1536 * g, 128), 1536)])
    top = swap(top)
    d_all[core, here] = top[:4].astype(BF)
    d_s[...] = top[4:].astype(BF)
    for dz, dy in plane + [(0, 0)]:
        if dz or dy:
            send(d_all.at[core, here], d_all.at[core, here], ST_D, in_plane(dz, dy))
        send(d_s, d_all.at[core, here], ST_D, beside(dz, dy))
    arrived(b_r, ST_D)
    top_bound = jnp.concatenate(
        [
            jnp.concatenate(
                [
                    swap(
                        jnp.concatenate(
                            [
                                d_all[h, 2 * j].astype(F32),
                                d_all[h, 2 * j + 1].astype(F32),
                            ],
                            axis=0,
                        )
                    )
                    for h in range(2)
                ],
                axis=0,
            ).astype(BF)
            for j in range(8)
        ],
        axis=1,
    )
    e_all[y] = (pre_mid[...] + nt(top_bound, d2[:, 512:])).astype(BF)
    for k in (2, 1, 3):
        send(e_all.at[y], e_all.at[y], ST_E, in_plane(0, k))
    arrived(a_r, ST_E)
    mid_bound = jnp.concatenate([e_all[j] for j in range(4)], axis=1)
    lb_ref[...] = (pre_leaf[...] + nt(mid_bound, joint[...])).astype(BF)

    sent(a_r, ST_A)
    sent(ai_r, ST_AI)
    sent(b_r, ST_B)
    sent(bi_r, ST_BI)
    sent(b2_r, ST_B2)
    sent(c1_r, ST_C1)
    sent(c2_r, ST_C2)
    for n in range(4):
        sent(c1_r.at[: 4 if n < 3 else 3], ST_C3 + n)
    sent(ur.at[64:], ST_UR)
    sent(dr.at[64:], ST_DR)
    sent(b_r, ST_D)
    sent(a_r, ST_E)


def lift(lb_ref, part_ref, ll_ref, out_ref):
    low = lax.broadcasted_iota(jnp.int32, (R, 128), 1) < 64
    zero = jnp.zeros((R, 128), BF)
    for m in range(8):
        pair = lb_ref[:, 128 * m : 128 * m + 128]
        both = jnp.concatenate(
            [jnp.where(low, pair, zero), jnp.where(low, zero, pair)], axis=0
        )
        lifted = nn(both, ll_ref[128 * m : 128 * m + 128, :])
        out_ref[:, 2 * m, :] = lifted[:16] + part_ref[2 * m]
        out_ref[:, 2 * m + 1, :] = lifted[16:] + part_ref[2 * m + 1]


def per_device(src, lf, lp, ll, bu, bd, u1, d1, u2, d2, ur, dr):
    args = (src, lf, lp, bu, bd, u1, d1, u2, d2, ur, dr)
    vmem = pl.BlockSpec(memory_space=pltpu.VMEM)
    lb, part = pl.pallas_call(
        kernel,
        out_shape=(
            jax.ShapeDtypeStruct((R, 1024), BF),
            jax.ShapeDtypeStruct((LEAF, R, 256), F32),
        ),
        in_specs=[pl.BlockSpec(memory_space=pltpu.HBM)] * 11,
        out_specs=(vmem, vmem),
        scratch_shapes=[pltpu.VMEM(a.shape, BF) for a in args[:-2]]
        + [pltpu.VMEM((128, 6144), BF)] * 2
        + [
            pltpu.VMEM((256, 256), BF),
            pltpu.VMEM((16, 1024), F32),
            pltpu.VMEM((16, 128), F32),
            pltpu.VMEM((1024, 512), BF),
            pltpu.VMEM((4, 16, 128), BF),
            pltpu.VMEM((3, 16, 128), BF),
            pltpu.VMEM((16, 256), BF),
            pltpu.VMEM((3, 16, 256), BF),
            pltpu.VMEM((2, 16, 4, 128), BF),
            pltpu.VMEM((31, 4, 128), BF),
            pltpu.VMEM((8, 8, 128), BF),
            pltpu.VMEM((15, 8, 128), BF),
            pltpu.VMEM((8, 8, 128), BF),
            pltpu.VMEM((7, 8, 128), BF),
            pltpu.VMEM((16, 8, 384), BF),
            pltpu.VMEM((15, 8, 384), BF),
            pltpu.VMEM((8, 384), BF),
            pltpu.VMEM((7, 8, 384), BF),
            pltpu.VMEM((16, 8, 384), BF),
            pltpu.VMEM((4, 128), BF),
            pltpu.VMEM((2, 16, 4, 128), BF),
            pltpu.VMEM((4, 16, 128), BF),
            pltpu.SemaphoreType.DMA((12,)),
            pltpu.SemaphoreType.DMA((N_STAGE,)),
            pltpu.SemaphoreType.DMA((N_STAGE,)),
            pltpu.SemaphoreType.REGULAR((3,)),
        ],
        compiler_params=pltpu.CompilerParams(
            collective_id=0, has_side_effects=True, vmem_limit_bytes=32 * 1024 * 1024
        ),
    )(*[pltpu.with_memory_space_constraint(a, pltpu.HBM) for a in args])
    return pl.pallas_call(
        lift,
        out_shape=jax.ShapeDtypeStruct((R, LEAF, 256), F32),
        in_specs=[vmem] * 3,
        out_specs=vmem,
        compiler_params=pltpu.CompilerParams(vmem_limit_bytes=8 * 1024 * 1024),
    )(lb, part, ll)


def solution(mesh):
    both = ("gx", "gy")
    return jax.shard_map(
        per_device,
        mesh=mesh,
        in_specs=(P(None, both, None),) + (P(both, None),) * 11,
        out_specs=P(None, both, None),
        check_vma=False,
    )
```

```python
import jax
import jax.numpy as jnp
from jax import lax
from jax.experimental import pallas as pl
from jax.experimental.pallas import tpu as pltpu
from jax.sharding import PartitionSpec as P

MESH = pl.DeviceIdType.MESH
BF = jnp.bfloat16
F32 = jnp.float32

R = 16
LEAF = 16
ST_A, ST_AI, ST_B, ST_BI, ST_B2, ST_C1, ST_C2, ST_D, ST_E, ST_UR, ST_DR = range(11)
ST_C3, ST_B3, ST_BX, ST_DX = 11, 15, 16, 17
N_STAGE = 18


def nt(x, w):
    return lax.dot_general(x, w, (((1,), (1,)), ((), ())), preferred_element_type=F32)


def nn(x, w):
    return jnp.dot(x, w, preferred_element_type=F32)


def kernel(
    src_h, lf_h, lp_h, bu_h, bd_h, u1_h, d1_h, u2_h, d2_h, ur_h, dr_h,
    lb_ref, part,
    src, lf, lp, bu, bd, u1, d1, u2, d2, ur, dr,
    sp, pre_leaf, pre_mid, joint,
    a_s, a_r, ai_s, ai_r,
    b_s, b_r, bx_s, bx_r, bi_s, bi_r, b2_s, b2_r, si,
    c1_s, c1_r, c2_s, c2_r, rs,
    d_s, d_all, e_all,
    load_sem, send_sem, recv_sem, round_sem,
):
    gx = lax.axis_index("gx")
    gy = lax.axis_index("gy")
    x, core = gx // 2, gx % 2
    y, z = gy % 4, gy // 4
    zl, zh = z % 4, z // 4

    pairs = (
        (src_h, src), (lf_h, lf), (bu_h.at[384:], bu.at[384:]), (u1_h, u1),
        (u2_h, u2), (ur_h, ur.at[:64]), (bu_h.at[:384], bu.at[:384]), (lp_h, lp),
        (bd_h, bd), (d1_h, d1), (d2_h, d2), (dr_h, dr.at[:64]),
    )
    loads = [
        pltpu.make_async_copy(h, v, load_sem.at[i]) for i, (h, v) in enumerate(pairs)
    ]
    (l_src, l_lf, l_bu, l_u1, l_u2, l_ur, l_bi, l_lp, l_bd, l_d1, l_d2, l_dr) = loads
    for l in loads[:4]:
        l.start()

    sibling = (x * 2 + 1 - core, gy)

    def across(dx, dy):
        return ((x + dx) % 4 * 2 + core, z * 4 + (y + dy) % 4)

    def in_plane(dz, dy):
        return (gx, (zh * 4 + (zl + dz) % 4) * 4 + (y + dy) % 4)

    def along_z(dz):
        return (gx, ((z + dz) % 8) * 4 + y)

    x_near = [across(1, 0), across(3, 0)]
    z_near = [along_z(1), along_z(7)]
    greet = [in_plane(0, k) for k in (2, 1, 3)] + [sibling] + z_near + x_near
    rounds = (z_near, z_near + x_near, z_near + x_near)
    barrier = pltpu.get_barrier_semaphore()
    for device in greet:
        pl.semaphore_signal(barrier, inc=1, device_id=device, device_id_type=MESH)

    def pass_on(n):
        if n == 0:
            pl.semaphore_wait(barrier, len(greet))
        else:
            pl.semaphore_wait(round_sem.at[n - 1], len(rounds[n - 1]))
        if n < 3:
            for device in rounds[n]:
                pl.semaphore_signal(
                    round_sem.at[n], inc=1, device_id=device, device_id_type=MESH
                )

    plane = [(dz, dy) for dz in (2, 3, 1, 0) for dy in (2, 1, 3, 0) if dz or dy]

    def send(s, d, stage, device):
        c = pltpu.make_async_remote_copy(
            src_ref=s,
            dst_ref=d,
            send_sem=send_sem.at[stage],
            recv_sem=recv_sem.at[stage],
            device_id=device,
            device_id_type=MESH,
        )
        c.start()

    def arrived(ref, stage):
        pltpu.make_async_copy(ref, ref, recv_sem.at[stage]).wait()

    def sent(ref, stage):
        pltpu.make_async_copy(ref, ref, send_sem.at[stage]).wait()

    l_src.wait()
    rows = lax.broadcasted_iota(jnp.int32, (256, 256), 0)
    cols = lax.broadcasted_iota(jnp.int32, (256, 256), 1)
    pick = ((rows % 16) * 16 + rows // 16 == cols).astype(F32).astype(BF)
    sp[...] = nn(pick, src[...].reshape(R * LEAF, 256)).astype(BF)
    quarter = lax.broadcasted_iota(jnp.int32, (8, 128), 0) < 4
    keep = quarter == (lax.broadcasted_iota(jnp.int32, (8, 128), 1) < 64)

    def swap(v):
        return jnp.where(keep, v, pltpu.roll(pltpu.roll(v, 64, 1), 4, 0))

    l_lf.wait()
    lane = lax.broadcasted_iota(jnp.int32, (R, 128), 1)
    blocks = []
    for m in range(8):
        f = nt(sp[32 * m : 32 * m + 32, :], lf[128 * m : 128 * m + 128, :])
        blocks.append(jnp.where(lane < 64, f[:16], f[16:]).astype(BF))
    flux = jnp.concatenate(blocks, axis=1)
    pass_on(0)
    send(ur_h, ur.at[64:], ST_UR, sibling)
    send(dr_h, dr.at[64:], ST_DR, sibling)
    l_bu.wait()
    box_flux = nt(flux, bu[384:, :]).astype(BF)
    l_u1.wait()
    for l in loads[4:]:
        l.start()
    first_flux = nn(box_flux, u1[:, 256:])
    for j in range(4):
        a_s[j] = first_flux[:, 128 * j : 128 * j + 128].astype(BF)
    for k in (2, 1, 3):
        send(a_s.at[(y + k) % 4], a_r.at[k - 1], ST_A, in_plane(0, k))
    pass_on(1)
    first_if = nn(box_flux, u1[:, :256])
    ai_s[...] = first_if.astype(BF)
    for k in (2, 1, 3):
        send(ai_s, ai_r.at[k - 1], ST_AI, in_plane(0, k))
    pass_on(2)
    l_u2.wait()

    arrived(a_r, ST_A)
    piece = a_s[y].astype(F32)
    for k in range(3):
        piece = piece + a_r[k].astype(F32)
    second_piece = piece.astype(BF)
    second_flux = nn(second_piece, u2[:, 512:])
    for j in range(8):
        for h in range(2):
            v = swap(second_flux[8 * h : 8 * h + 8, 128 * j : 128 * j + 128])
            b_s[2 * j, h] = v[:4].astype(BF)
            b_s[2 * j + 1, h] = v[4:].astype(BF)
    pass_on(3)
    for dz, dy in plane:
        to = (zl + dz) % 4 * 4 + (y + dy) % 4
        send(b_s.at[to], b_r.at[dz * 4 + dy - 1], ST_B, in_plane(dz, dy))
    second_if = nn(second_piece, u2[:, :512])
    for j in range(4):
        bi_s[j] = second_if[:, 128 * j : 128 * j + 128].astype(BF)
    for k in (2, 1, 3):
        send(bi_s.at[(y + k) % 4], bi_r.at[k - 1], ST_BI, in_plane(0, k))
    l_bi.wait()
    box_if = nt(flux, bu[:384, :]).astype(BF)
    l_ur.wait()

    arrived(b_r, ST_B)
    here = zl * 4 + y
    for h in range(2):
        total = b_s[here, h].astype(F32)
        for k in range(15):
            total = total + b_r[k, h].astype(F32)
        bx_s[h] = total.astype(BF)
    send(bx_s.at[1 - core], bx_r, ST_BX, sibling)
    arrived(bx_r, ST_BX)
    root_piece = swap(
        jnp.concatenate([bx_s[core].astype(F32), bx_r[...].astype(F32)], axis=0)
    ).astype(BF)
    arrived(ur.at[64:], ST_UR)
    for j in range(16):
        c1_s[j] = nn(root_piece, ur[:, 384 * j : 384 * j + 384]).astype(BF)
    reach = (2, 1, 3, 0)
    for dx in reach:
        for dy in reach:
            if dx or dy:
                send(
                    c1_s.at[(x + dx) % 4 * 4 + (y + dy) % 4],
                    c1_r.at[dx * 4 + dy - 1],
                    ST_C1,
                    across(dx, dy),
                )
    arrived(bi_r, ST_BI)
    block = bi_s[y].astype(F32)
    for k in range(3):
        block = block + bi_r[k].astype(F32)
    b2_s[...] = block.astype(BF)
    for dz in (2, 3, 1):
        send(b2_s, b2_r.at[dz - 1], ST_B2, in_plane(dz, 0))
    l_lp.wait()
    for l in range(LEAF):
        part[l] = nn(sp[16 * l : 16 * l + 16, :], lp[256 * l : 256 * l + 256, :])
    arrived(ai_r, ST_AI)
    whole = ai_s[...].astype(F32)
    for k in range(3):
        whole = whole + ai_r[k].astype(F32)
    l_d1.wait()
    l_bd.wait()
    box_part = nt(whole.astype(BF), d1[:, :256]).astype(BF)
    pre_leaf[...] = nt(box_if, bd[:, :384]) + nt(box_part, bd[:, 384:])
    l_d2.wait()
    l_dr.wait()

    arrived(c1_r, ST_C1)
    corner = x * 4 + y
    mine = c1_s[corner].astype(F32)
    for k in range(15):
        mine = mine + c1_r[k].astype(F32)
    c2_s[...] = mine.astype(BF)
    for dz in (4, 3, 5, 2, 6, 1, 7):
        send(c2_s, c2_r.at[dz - 1], ST_C2, along_z(dz))
    arrived(b2_r, ST_B2)
    for k in range(3):
        block = block + b2_r[k].astype(F32)
    si[y] = block.astype(BF)
    for k in (2, 1, 3):
        send(si.at[y], si.at[y], ST_B3, in_plane(0, k))

    arrived(c2_r, ST_C2)
    for k in range(7):
        mine = mine + c2_r[k].astype(F32)
    rs[corner] = mine.astype(BF)
    for n, dx in enumerate(reach):
        for dy in (2, 1, 3, 0):
            if dx or dy:
                send(rs.at[corner], rs.at[corner], ST_C3 + n, across(dx, dy))
    for h in range(2):
        joint[:, 256 * h : 256 * h + 256] = nn(
            bd[:, 384:], d1[:, 256 + 256 * h : 512 + 256 * h]
        ).astype(BF)
    arrived(bi_r, ST_B3)
    second_iface = jnp.concatenate([si[j] for j in range(4)], axis=1)
    pre_mid[...] = nt(second_iface, d2[:, :512])
    arrived(dr.at[64:], ST_DR)
    top = jnp.zeros((8, 128), F32)
    for n in (3, 1, 2, 0):
        g = (x + 4 - reach[n]) % 4
        arrived(c1_r.at[: 4 if n < 3 else 3], ST_C3 + n)
        v = jnp.concatenate([rs[4 * g + q] for q in range(4)], axis=1)
        top = top + nt(v, dr[:, pl.ds(pl.multiple_of(1536 * g, 128), 1536)])
    top = swap(top)
    d_all[here, core] = top[:4].astype(BF)
    d_s[...] = top[4:].astype(BF)
    send(d_s, d_all.at[here, core], ST_DX, sibling)
    arrived(d_s, ST_DX)
    for dz, dy in plane:
        send(d_all.at[here], d_all.at[here], ST_D, in_plane(dz, dy))
    arrived(b_r, ST_D)
    top_bound = jnp.concatenate(
        [
            jnp.concatenate(
                [
                    swap(
                        jnp.concatenate(
                            [
                                d_all[2 * j, h].astype(F32),
                                d_all[2 * j + 1, h].astype(F32),
                            ],
                            axis=0,
                        )
                    )
                    for h in range(2)
                ],
                axis=0,
            ).astype(BF)
            for j in range(8)
        ],
        axis=1,
    )
    e_all[y] = (pre_mid[...] + nt(top_bound, d2[:, 512:])).astype(BF)
    for k in (2, 1, 3):
        send(e_all.at[y], e_all.at[y], ST_E, in_plane(0, k))
    arrived(a_r, ST_E)
    mid_bound = jnp.concatenate([e_all[j] for j in range(4)], axis=1)
    lb_ref[...] = (pre_leaf[...] + nt(mid_bound, joint[...])).astype(BF)

    sent(a_r, ST_A)
    sent(ai_r, ST_AI)
    sent(b_r, ST_B)
    sent(bi_r, ST_BI)
    sent(b2_r, ST_B2)
    sent(bi_r, ST_B3)
    sent(bx_r, ST_BX)
    sent(d_s, ST_DX)
    sent(c1_r, ST_C1)
    sent(c2_r, ST_C2)
    for n in range(4):
        sent(c1_r.at[: 4 if n < 3 else 3], ST_C3 + n)
    sent(ur.at[64:], ST_UR)
    sent(dr.at[64:], ST_DR)
    sent(b_r, ST_D)
    sent(a_r, ST_E)


def lift(lb_ref, part_ref, ll_ref, out_ref):
    low = lax.broadcasted_iota(jnp.int32, (R, 128), 1) < 64
    zero = jnp.zeros((R, 128), BF)
    for m in range(8):
        pair = lb_ref[:, 128 * m : 128 * m + 128]
        both = jnp.concatenate(
            [jnp.where(low, pair, zero), jnp.where(low, zero, pair)], axis=0
        )
        lifted = nn(both, ll_ref[128 * m : 128 * m + 128, :])
        out_ref[:, 2 * m, :] = lifted[:16] + part_ref[2 * m]
        out_ref[:, 2 * m + 1, :] = lifted[16:] + part_ref[2 * m + 1]


def per_device(src, lf, lp, ll, bu, bd, u1, d1, u2, d2, ur, dr):
    args = (src, lf, lp, bu, bd, u1, d1, u2, d2, ur, dr)
    vmem = pl.BlockSpec(memory_space=pltpu.VMEM)
    lb, part = pl.pallas_call(
        kernel,
        out_shape=(
            jax.ShapeDtypeStruct((R, 1024), BF),
            jax.ShapeDtypeStruct((LEAF, R, 256), F32),
        ),
        in_specs=[pl.BlockSpec(memory_space=pltpu.HBM)] * 11,
        out_specs=(vmem, vmem),
        scratch_shapes=[pltpu.VMEM(a.shape, BF) for a in args[:-2]]
        + [pltpu.VMEM((128, 6144), BF)] * 2
        + [
            pltpu.VMEM((256, 256), BF),
            pltpu.VMEM((16, 1024), F32),
            pltpu.VMEM((16, 128), F32),
            pltpu.VMEM((1024, 512), BF),
            pltpu.VMEM((4, 16, 128), BF),
            pltpu.VMEM((3, 16, 128), BF),
            pltpu.VMEM((16, 256), BF),
            pltpu.VMEM((3, 16, 256), BF),
            pltpu.VMEM((16, 2, 4, 128), BF),
            pltpu.VMEM((15, 2, 4, 128), BF),
            pltpu.VMEM((2, 4, 128), BF),
            pltpu.VMEM((4, 128), BF),
            pltpu.VMEM((4, 16, 128), BF),
            pltpu.VMEM((3, 16, 128), BF),
            pltpu.VMEM((16, 128), BF),
            pltpu.VMEM((3, 16, 128), BF),
            pltpu.VMEM((4, 16, 128), BF),
            pltpu.VMEM((16, 8, 384), BF),
            pltpu.VMEM((15, 8, 384), BF),
            pltpu.VMEM((8, 384), BF),
            pltpu.VMEM((7, 8, 384), BF),
            pltpu.VMEM((16, 8, 384), BF),
            pltpu.VMEM((4, 128), BF),
            pltpu.VMEM((16, 2, 4, 128), BF),
            pltpu.VMEM((4, 16, 128), BF),
            pltpu.SemaphoreType.DMA((12,)),
            pltpu.SemaphoreType.DMA((N_STAGE,)),
            pltpu.SemaphoreType.DMA((N_STAGE,)),
            pltpu.SemaphoreType.REGULAR((3,)),
        ],
        compiler_params=pltpu.CompilerParams(
            collective_id=0, has_side_effects=True, vmem_limit_bytes=32 * 1024 * 1024
        ),
    )(*[pltpu.with_memory_space_constraint(a, pltpu.HBM) for a in args])
    return pl.pallas_call(
        lift,
        out_shape=jax.ShapeDtypeStruct((R, LEAF, 256), F32),
        in_specs=[vmem] * 3,
        out_specs=vmem,
        compiler_params=pltpu.CompilerParams(vmem_limit_bytes=8 * 1024 * 1024),
    )(lb, part, ll)


def solution(mesh):
    both = ("gx", "gy")
    return jax.shard_map(
        per_device,
        mesh=mesh,
        in_specs=(P(None, both, None),) + (P(both, None),) * 11,
        out_specs=P(None, both, None),
        check_vma=False,
    )
```

```python
import jax
import jax.numpy as jnp
from jax import lax
from jax.experimental import pallas as pl
from jax.experimental.pallas import tpu as pltpu
from jax.sharding import PartitionSpec as P

MESH = pl.DeviceIdType.MESH
BF = jnp.bfloat16
F32 = jnp.float32

R = 16
LEAF = 16
ST_A, ST_AI, ST_B, ST_BI, ST_B2, ST_C1, ST_C2, ST_D, ST_E, ST_UR, ST_DR = range(11)
ST_C3, ST_B3, ST_U2, ST_D2 = 11, 15, 16, 17
N_STAGE = 18


def nt(x, w):
    return lax.dot_general(x, w, (((1,), (1,)), ((), ())), preferred_element_type=F32)


def nn(x, w):
    return jnp.dot(x, w, preferred_element_type=F32)


def kernel(
    src_h, lf_h, lp_h, bu_h, bd_h, u1_h, d1_h, u2_h, d2_h, ur_h, dr_h,
    lb_ref, part,
    src, lf, lp, bu, bd, u1, d1, u2, d2, ur, dr,
    sp, pre_leaf, pre_mid, joint,
    a_s, a_r, ai_s, ai_r,
    b_s, b_r, bi_s, bi_r, b2_s, b2_r, si,
    c1_s, c1_r, c2_s, c2_r, rs,
    d_all, e_s, e_all,
    load_sem, send_sem, recv_sem, round_sem,
):
    gx = lax.axis_index("gx")
    gy = lax.axis_index("gy")
    x, core = gx // 2, gx % 2
    y, z = gy % 4, gy // 4
    zl, zh = z % 4, z // 4

    pairs = (
        (src_h, src), (lf_h, lf), (bu_h.at[384:], bu.at[384:]), (u1_h, u1),
        (u2_h, u2.at[:128]), (ur_h, ur.at[:64]), (bu_h.at[:384], bu.at[:384]), (lp_h, lp),
        (bd_h, bd), (d1_h, d1), (d2_h, d2.at[:128]), (dr_h, dr.at[:64]),
    )
    loads = [
        pltpu.make_async_copy(h, v, load_sem.at[i]) for i, (h, v) in enumerate(pairs)
    ]
    (l_src, l_lf, l_bu, l_u1, l_u2, l_ur, l_bi, l_lp, l_bd, l_d1, l_d2, l_dr) = loads
    for l in loads[:4]:
        l.start()

    sibling = (x * 2 + 1 - core, gy)

    def across(dx, dy):
        return ((x + dx) % 4 * 2 + core, z * 4 + (y + dy) % 4)

    def in_plane(dz, dy):
        return (gx, (zh * 4 + (zl + dz) % 4) * 4 + (y + dy) % 4)

    def beside(dy):
        return (sibling[0], z * 4 + (y + dy) % 4)

    def along_z(dz):
        return (gx, ((z + dz) % 8) * 4 + y)

    x_near = [across(1, 0), across(3, 0)]
    z_near = [along_z(1), along_z(7)]
    greet = [in_plane(0, k) for k in (2, 1, 3)] + [beside(k) for k in (2, 1, 3, 0)]
    greet += z_near + x_near
    rounds = (z_near, z_near + x_near, z_near + x_near)
    barrier = pltpu.get_barrier_semaphore()
    for device in greet:
        pl.semaphore_signal(barrier, inc=1, device_id=device, device_id_type=MESH)

    def pass_on(n):
        if n == 0:
            pl.semaphore_wait(barrier, len(greet))
        else:
            pl.semaphore_wait(round_sem.at[n - 1], len(rounds[n - 1]))
        if n < 3:
            for device in rounds[n]:
                pl.semaphore_signal(
                    round_sem.at[n], inc=1, device_id=device, device_id_type=MESH
                )

    plane = [(dz, dy) for dz in (2, 3, 1, 0) for dy in (2, 1, 3, 0) if dz or dy]

    def send(s, d, stage, device):
        c = pltpu.make_async_remote_copy(
            src_ref=s,
            dst_ref=d,
            send_sem=send_sem.at[stage],
            recv_sem=recv_sem.at[stage],
            device_id=device,
            device_id_type=MESH,
        )
        c.start()

    def arrived(ref, stage):
        pltpu.make_async_copy(ref, ref, recv_sem.at[stage]).wait()

    def sent(ref, stage):
        pltpu.make_async_copy(ref, ref, send_sem.at[stage]).wait()

    l_src.wait()
    rows = lax.broadcasted_iota(jnp.int32, (256, 256), 0)
    cols = lax.broadcasted_iota(jnp.int32, (256, 256), 1)
    pick = ((rows % 16) * 16 + rows // 16 == cols).astype(F32).astype(BF)
    sp[...] = nn(pick, src[...].reshape(R * LEAF, 256)).astype(BF)
    low = lax.broadcasted_iota(jnp.int32, (8, 128), 1) < 64

    def weave(a, b):
        return (
            jnp.where(low, a, pltpu.roll(b, 64, 1)),
            jnp.where(low, pltpu.roll(a, 64, 1), b),
        )

    l_lf.wait()
    lane = lax.broadcasted_iota(jnp.int32, (R, 128), 1)
    blocks = []
    for m in range(8):
        f = nt(sp[32 * m : 32 * m + 32, :], lf[128 * m : 128 * m + 128, :])
        blocks.append(jnp.where(lane < 64, f[:16], f[16:]).astype(BF))
    flux = jnp.concatenate(blocks, axis=1)
    pass_on(0)
    send(u2_h, u2.at[128:], ST_U2, sibling)
    send(ur_h, ur.at[64:], ST_UR, sibling)
    send(d2_h, d2.at[128:], ST_D2, sibling)
    send(dr_h, dr.at[64:], ST_DR, sibling)
    l_bu.wait()
    box_flux = nt(flux, bu[384:, :]).astype(BF)
    l_u1.wait()
    for l in loads[4:]:
        l.start()
    first_flux = nn(box_flux, u1[:, 256:])
    for j in range(4):
        for h in range(2):
            a_s[h, j] = first_flux[8 * h : 8 * h + 8, 128 * j : 128 * j + 128].astype(BF)
    for k in (2, 1, 3, 0):
        if k:
            send(a_s.at[core, (y + k) % 4], a_r.at[k - 1], ST_A, in_plane(0, k))
        send(a_s.at[1 - core, (y + k) % 4], a_r.at[3 + k], ST_A, beside(k))
    pass_on(1)
    first_if = nn(box_flux, u1[:, :256])
    ai_s[...] = first_if.astype(BF)
    for k in (2, 1, 3):
        send(ai_s, ai_r.at[k - 1], ST_AI, in_plane(0, k))
    pass_on(2)
    l_u2.wait()

    arrived(a_r, ST_A)
    piece = a_s[core, y].astype(F32)
    other = a_r[3].astype(F32)
    for k in range(3):
        piece = piece + a_r[k].astype(F32)
        other = other + a_r[4 + k].astype(F32)
    piece, other = piece.astype(BF), other.astype(BF)
    arrived(u2.at[128:], ST_U2)
    mine2 = nn(piece, u2[:128, 512:])
    other2 = nn(other, u2[128:, 512:])
    for j in range(8):
        cut = slice(128 * j, 128 * j + 128)
        even, odd = weave(mine2[:, cut], other2[:, cut])
        b_s[2 * j] = even.astype(BF)
        b_s[2 * j + 1] = odd.astype(BF)
    pass_on(3)
    for dz, dy in plane:
        to = (zl + dz) % 4 * 4 + (y + dy) % 4
        send(b_s.at[to], b_r.at[dz * 4 + dy - 1], ST_B, in_plane(dz, dy))
    mine_if = nn(piece, u2[:128, :512])
    other_if = nn(other, u2[128:, :512])
    for j in range(4):
        bi_s[j, 0] = mine_if[:, 128 * j : 128 * j + 128].astype(BF)
        bi_s[j, 1] = other_if[:, 128 * j : 128 * j + 128].astype(BF)
    for k in (2, 1, 3):
        send(bi_s.at[(y + k) % 4], bi_r.at[k - 1], ST_BI, in_plane(0, k))
    l_bi.wait()
    box_if = nt(flux, bu[:384, :]).astype(BF)
    l_ur.wait()

    arrived(b_r, ST_B)
    here = zl * 4 + y
    total = b_s[here].astype(F32)
    for k in range(15):
        total = total + b_r[k].astype(F32)
    root_piece = total.astype(BF)
    arrived(ur.at[64:], ST_UR)
    for j in range(16):
        c1_s[j] = nn(root_piece, ur[:, 384 * j : 384 * j + 384]).astype(BF)
    reach = (2, 1, 3, 0)
    for dx in reach:
        for dy in reach:
            if dx or dy:
                send(
                    c1_s.at[(x + dx) % 4 * 4 + (y + dy) % 4],
                    c1_r.at[dx * 4 + dy - 1],
                    ST_C1,
                    across(dx, dy),
                )
    arrived(bi_r, ST_BI)
    block = bi_s[y].astype(F32)
    for k in range(3):
        block = block + bi_r[k].astype(F32)
    b2_s[...] = block.astype(BF)
    for dz in (2, 3, 1):
        send(b2_s, b2_r.at[dz - 1], ST_B2, in_plane(dz, 0))
    l_lp.wait()
    for l in range(LEAF):
        part[l] = nn(sp[16 * l : 16 * l + 16, :], lp[256 * l : 256 * l + 256, :])
    arrived(ai_r, ST_AI)
    whole = ai_s[...].astype(F32)
    for k in range(3):
        whole = whole + ai_r[k].astype(F32)
    l_d1.wait()
    l_bd.wait()
    box_part = nt(whole.astype(BF), d1[:, :256]).astype(BF)
    pre_leaf[...] = nt(box_if, bd[:, :384]) + nt(box_part, bd[:, 384:])
    l_d2.wait()
    l_dr.wait()

    arrived(c1_r, ST_C1)
    corner = x * 4 + y
    mine = c1_s[corner].astype(F32)
    for k in range(15):
        mine = mine + c1_r[k].astype(F32)
    c2_s[...] = mine.astype(BF)
    for dz in (4, 3, 5, 2, 6, 1, 7):
        send(c2_s, c2_r.at[dz - 1], ST_C2, along_z(dz))
    arrived(b2_r, ST_B2)
    for k in range(3):
        block = block + b2_r[k].astype(F32)
    si[y] = block.astype(BF)
    for k in (2, 1, 3):
        send(si.at[y], si.at[y], ST_B3, in_plane(0, k))

    arrived(c2_r, ST_C2)
    for k in range(7):
        mine = mine + c2_r[k].astype(F32)
    rs[corner] = mine.astype(BF)
    for n, dx in enumerate(reach):
        for dy in (2, 1, 3, 0):
            if dx or dy:
                send(rs.at[corner], rs.at[corner], ST_C3 + n, across(dx, dy))
    for h in range(2):
        joint[:, 256 * h : 256 * h + 256] = nn(
            bd[:, 384:], d1[:, 256 + 256 * h : 512 + 256 * h]
        ).astype(BF)
    arrived(bi_r, ST_B3)
    arrived(d2.at[128:], ST_D2)
    for h in range(2):
        second_iface = jnp.concatenate([si[j, h] for j in range(4)], axis=1)
        pre_mid[h] = nt(second_iface, d2[128 * h : 128 * h + 128, :512])
    arrived(dr.at[64:], ST_DR)
    top = jnp.zeros((8, 128), F32)
    for n in (3, 1, 2, 0):
        g = (x + 4 - reach[n]) % 4
        arrived(c1_r.at[: 4 if n < 3 else 3], ST_C3 + n)
        v = jnp.concatenate([rs[4 * g + q] for q in range(4)], axis=1)
        top = top + nt(v, dr[:, pl.ds(pl.multiple_of(1536 * g, 128), 1536)])
    d_all[here] = top.astype(BF)
    for dz, dy in plane:
        send(d_all.at[here], d_all.at[here], ST_D, in_plane(dz, dy))
    arrived(b_r, ST_D)
    pairs = [
        weave(d_all[2 * j].astype(F32), d_all[2 * j + 1].astype(F32)) for j in range(8)
    ]
    mids = []
    for h in range(2):
        bound = jnp.concatenate([p[h] for p in pairs], axis=1).astype(BF)
        mids.append(
            (pre_mid[h] + nt(bound, d2[128 * h : 128 * h + 128, 512:])).astype(BF)
        )
    e_all[core, y] = mids[0]
    e_s[...] = mids[1]
    for k in (2, 1, 3, 0):
        if k:
            send(e_all.at[core, y], e_all.at[core, y], ST_E, in_plane(0, k))
        send(e_s, e_all.at[core, y], ST_E, beside(k))
    arrived(a_r, ST_E)
    mid_bound = jnp.concatenate(
        [
            jnp.concatenate(
                [e_all[0, j].astype(F32), e_all[1, j].astype(F32)], axis=0
            ).astype(BF)
            for j in range(4)
        ],
        axis=1,
    )
    lb_ref[...] = (pre_leaf[...] + nt(mid_bound, joint[...])).astype(BF)

    sent(a_r, ST_A)
    sent(ai_r, ST_AI)
    sent(b_r, ST_B)
    sent(bi_r, ST_BI)
    sent(b2_r, ST_B2)
    sent(bi_r, ST_B3)
    sent(u2.at[128:], ST_U2)
    sent(d2.at[128:], ST_D2)
    sent(c1_r, ST_C1)
    sent(c2_r, ST_C2)
    for n in range(4):
        sent(c1_r.at[: 4 if n < 3 else 3], ST_C3 + n)
    sent(ur.at[64:], ST_UR)
    sent(dr.at[64:], ST_DR)
    sent(b_r, ST_D)
    sent(a_r, ST_E)


def lift(lb_ref, part_ref, ll_ref, out_ref):
    low = lax.broadcasted_iota(jnp.int32, (R, 128), 1) < 64
    zero = jnp.zeros((R, 128), BF)
    for m in range(8):
        pair = lb_ref[:, 128 * m : 128 * m + 128]
        both = jnp.concatenate(
            [jnp.where(low, pair, zero), jnp.where(low, zero, pair)], axis=0
        )
        lifted = nn(both, ll_ref[128 * m : 128 * m + 128, :])
        out_ref[:, 2 * m, :] = lifted[:16] + part_ref[2 * m]
        out_ref[:, 2 * m + 1, :] = lifted[16:] + part_ref[2 * m + 1]


def per_device(src, lf, lp, ll, bu, bd, u1, d1, u2, d2, ur, dr):
    args = (src, lf, lp, bu, bd, u1, d1, u2, d2, ur, dr)
    vmem = pl.BlockSpec(memory_space=pltpu.VMEM)
    lb, part = pl.pallas_call(
        kernel,
        out_shape=(
            jax.ShapeDtypeStruct((R, 1024), BF),
            jax.ShapeDtypeStruct((LEAF, R, 256), F32),
        ),
        in_specs=[pl.BlockSpec(memory_space=pltpu.HBM)] * 11,
        out_specs=(vmem, vmem),
        scratch_shapes=[pltpu.VMEM(a.shape, BF) for a in args[:-4]]
        + [pltpu.VMEM((2 * a.shape[0], a.shape[1]), BF) for a in args[-4:]]
        + [
            pltpu.VMEM((256, 256), BF),
            pltpu.VMEM((16, 1024), F32),
            pltpu.VMEM((2, 8, 128), F32),
            pltpu.VMEM((1024, 512), BF),
            pltpu.VMEM((2, 4, 8, 128), BF),
            pltpu.VMEM((7, 8, 128), BF),
            pltpu.VMEM((16, 256), BF),
            pltpu.VMEM((3, 16, 256), BF),
            pltpu.VMEM((16, 8, 128), BF),
            pltpu.VMEM((15, 8, 128), BF),
            pltpu.VMEM((4, 2, 8, 128), BF),
            pltpu.VMEM((3, 2, 8, 128), BF),
            pltpu.VMEM((2, 8, 128), BF),
            pltpu.VMEM((3, 2, 8, 128), BF),
            pltpu.VMEM((4, 2, 8, 128), BF),
            pltpu.VMEM((16, 8, 384), BF),
            pltpu.VMEM((15, 8, 384), BF),
            pltpu.VMEM((8, 384), BF),
            pltpu.VMEM((7, 8, 384), BF),
            pltpu.VMEM((16, 8, 384), BF),
            pltpu.VMEM((16, 8, 128), BF),
            pltpu.VMEM((8, 128), BF),
            pltpu.VMEM((2, 4, 8, 128), BF),
            pltpu.SemaphoreType.DMA((12,)),
            pltpu.SemaphoreType.DMA((N_STAGE,)),
            pltpu.SemaphoreType.DMA((N_STAGE,)),
            pltpu.SemaphoreType.REGULAR((3,)),
        ],
        compiler_params=pltpu.CompilerParams(
            collective_id=0, has_side_effects=True, vmem_limit_bytes=32 * 1024 * 1024
        ),
    )(*[pltpu.with_memory_space_constraint(a, pltpu.HBM) for a in args])
    return pl.pallas_call(
        lift,
        out_shape=jax.ShapeDtypeStruct((R, LEAF, 256), F32),
        in_specs=[vmem] * 3,
        out_specs=vmem,
        compiler_params=pltpu.CompilerParams(vmem_limit_bytes=8 * 1024 * 1024),
    )(lb, part, ll)


def solution(mesh):
    both = ("gx", "gy")
    return jax.shard_map(
        per_device,
        mesh=mesh,
        in_specs=(P(None, both, None),) + (P(both, None),) * 11,
        out_specs=P(None, both, None),
        check_vma=False,
    )
```

```python
import jax
import jax.numpy as jnp
from jax import lax
from jax.experimental import pallas as pl
from jax.experimental.pallas import tpu as pltpu
from jax.sharding import PartitionSpec as P

MESH = pl.DeviceIdType.MESH
BF = jnp.bfloat16
F32 = jnp.float32

R = 16
LEAF = 16
ST_A, ST_AI, ST_B, ST_BI, ST_B2, ST_C1, ST_C2, ST_C3, ST_D, ST_E, ST_B3 = range(11)
N_STAGE = 11


def nt(x, w):
    return lax.dot_general(x, w, (((1,), (1,)), ((), ())), preferred_element_type=F32)


def nn(x, w):
    return jnp.dot(x, w, preferred_element_type=F32)


def kernel(
    src_h, lf_h, lp_h, bu_h, bd_h, u1_h, d1_h, u2_h, d2_h, ur_h, dr_h,
    lb_ref, part,
    src, lf, lp, bu, bd, u1, d1, u2, d2, ur, dr,
    sp, pre_leaf, pre_mid, joint,
    a_s, a_r, ai_s, ai_r,
    b_s, b_r, bi_s, bi_r, b2_s, b2_r, si,
    c1_s, c1_r, c2_s, c2_r, rs,
    d_all, e_all,
    load_sem, send_sem, recv_sem,
):
    gx = lax.axis_index("gx")
    gy = lax.axis_index("gy")
    x, core = gx // 2, gx % 2
    y, z = gy % 4, gy // 4
    zl, zh = z % 4, z // 4

    pairs = (
        (src_h, src), (lf_h, lf), (bu_h.at[384:], bu.at[384:]), (u1_h, u1),
        (u2_h, u2), (ur_h, ur), (bu_h.at[:384], bu.at[:384]), (lp_h, lp),
        (bd_h, bd), (d1_h, d1), (d2_h, d2), (dr_h, dr),
    )
    loads = [
        pltpu.make_async_copy(h, v, load_sem.at[i]) for i, (h, v) in enumerate(pairs)
    ]
    (l_src, l_lf, l_bu, l_u1, l_u2, l_ur, l_bi, l_lp, l_bd, l_d1, l_d2, l_dr) = loads
    for l in loads[:4]:
        l.start()

    def across(dx, dc, dy):
        return (((x + dx) % 4) * 2 + (core + dc) % 2, z * 4 + (y + dy) % 4)

    def in_plane(dz, dy):
        return (gx, (zh * 4 + (zl + dz) % 4) * 4 + (y + dy) % 4)

    def along_z(dz):
        return (gx, ((z + dz) % 8) * 4 + y)

    barrier = pltpu.get_barrier_semaphore()
    greet = [(gx, ((1 - zh) * 4 + far) * 4 + y) for far in range(4)]
    plane = [(dz, dy) for dz in (2, 3, 1, 0) for dy in (2, 1, 3, 0) if dz or dy]
    third = [
        (dx, dc, dy)
        for dx in (2, 1, 3, 0)
        for dy in (2, 1, 3, 0)
        for dc in (0, 1)
        if dx or dc or dy
    ]
    greet += [in_plane(dz, dy) for dz, dy in plane]
    greet += [across(dx, dc, dy) for dx, dc, dy in third if dx or dc]
    for device in greet:
        pl.semaphore_signal(barrier, inc=1, device_id=device, device_id_type=MESH)

    def send(s, d, stage, device):
        c = pltpu.make_async_remote_copy(
            src_ref=s,
            dst_ref=d,
            send_sem=send_sem.at[stage],
            recv_sem=recv_sem.at[stage],
            device_id=device,
            device_id_type=MESH,
        )
        c.start()

    def arrived(ref, stage):
        pltpu.make_async_copy(ref, ref, recv_sem.at[stage]).wait()

    def sent(ref, stage):
        pltpu.make_async_copy(ref, ref, send_sem.at[stage]).wait()

    l_src.wait()
    rows = lax.broadcasted_iota(jnp.int32, (256, 256), 0)
    cols = lax.broadcasted_iota(jnp.int32, (256, 256), 1)
    pick = ((rows % 16) * 16 + rows // 16 == cols).astype(F32).astype(BF)
    sp[...] = nn(pick, src[...].reshape(R * LEAF, 256)).astype(BF)
    l_lf.wait()
    lane = lax.broadcasted_iota(jnp.int32, (R, 128), 1)
    low = lax.broadcasted_iota(jnp.int32, (8, 128), 1) < 64

    def pack(v):
        up, down = v[:8], v[8:]
        first = jnp.where(low, up, pltpu.roll(down, 64, 1))
        second = jnp.where(low, pltpu.roll(up, 64, 1), down)
        return first.astype(BF), second.astype(BF)

    def unpack(first, second):
        first, second = first.astype(F32), second.astype(F32)
        up = jnp.where(low, first, pltpu.roll(second, 64, 1))
        down = jnp.where(low, pltpu.roll(first, 64, 1), second)
        return jnp.concatenate([up, down], axis=0).astype(BF)

    blocks = []
    for m in range(8):
        f = nt(sp[32 * m : 32 * m + 32, :], lf[128 * m : 128 * m + 128, :])
        blocks.append(jnp.where(lane < 64, f[:16], f[16:]).astype(BF))
    flux = jnp.concatenate(blocks, axis=1)
    l_bu.wait()
    box_flux = nt(flux, bu[384:, :]).astype(BF)
    l_u1.wait()
    for l in loads[4:]:
        l.start()
    first_flux = nn(box_flux, u1[:, 256:])
    for j in range(4):
        a_s[j] = first_flux[:, 128 * j : 128 * j + 128].astype(BF)
    pl.semaphore_wait(barrier, len(greet))
    for k in (2, 1, 3):
        send(a_s.at[(y + k) % 4], a_r.at[k - 1], ST_A, in_plane(0, k))
    first_if = nn(box_flux, u1[:, :256])
    ai_s[...] = first_if.astype(BF)
    for k in (2, 1, 3):
        send(ai_s, ai_r.at[k - 1], ST_AI, in_plane(0, k))
    l_u2.wait()

    arrived(a_r, ST_A)
    piece = a_s[y].astype(F32)
    for k in range(3):
        piece = piece + a_r[k].astype(F32)
    second_piece = piece.astype(BF)
    second_flux = nn(second_piece, u2[:, 512:])
    for j in range(8):
        b_s[2 * j], b_s[2 * j + 1] = pack(second_flux[:, 128 * j : 128 * j + 128])
    for dz, dy in plane:
        to = (zl + dz) % 4 * 4 + (y + dy) % 4
        send(b_s.at[to], b_r.at[dz * 4 + dy - 1], ST_B, in_plane(dz, dy))
    second_if = nn(second_piece, u2[:, :512])
    for j in range(4):
        bi_s[j] = second_if[:, 128 * j : 128 * j + 128].astype(BF)
    for k in (2, 1, 3):
        send(bi_s.at[(y + k) % 4], bi_r.at[k - 1], ST_BI, in_plane(0, k))
    l_bi.wait()
    box_if = nt(flux, bu[:384, :]).astype(BF)
    l_ur.wait()

    arrived(b_r, ST_B)
    here = zl * 4 + y
    total = b_s[here].astype(F32)
    for k in range(15):
        total = total + b_r[k].astype(F32)
    root_piece = jnp.concatenate([total[:, :64], total[:, 64:]], axis=0).astype(BF)
    for j in range(16):
        t = nn(root_piece, ur[:, 384 * j : 384 * j + 384])
        c1_s[0, j] = t[:8].astype(BF)
        c1_s[1, j] = t[8:].astype(BF)
    for dx, dc, dy in third:
        to = ((x + dx) % 4) * 4 + (y + dy) % 4
        send(
            c1_s.at[(core + dc) % 2, to],
            c1_r.at[(dx * 4 + dy) * 2 + dc - 1],
            ST_C1,
            across(dx, dc, dy),
        )
    arrived(bi_r, ST_BI)
    block = bi_s[y].astype(F32)
    for k in range(3):
        block = block + bi_r[k].astype(F32)
    b2_s[...] = block.astype(BF)
    for dz in (2, 3, 1):
        send(b2_s, b2_r.at[dz - 1], ST_B2, in_plane(dz, 0))
    l_lp.wait()
    for l in range(LEAF):
        part[l] = nn(sp[16 * l : 16 * l + 16, :], lp[256 * l : 256 * l + 256, :])
    arrived(ai_r, ST_AI)
    whole = ai_s[...].astype(F32)
    for k in range(3):
        whole = whole + ai_r[k].astype(F32)
    l_d1.wait()
    l_bd.wait()
    box_part = nt(whole.astype(BF), d1[:, :256]).astype(BF)
    pre_leaf[...] = nt(box_if, bd[:, :384]) + nt(box_part, bd[:, 384:])
    l_d2.wait()
    l_dr.wait()

    arrived(c1_r, ST_C1)
    mine = c1_s[core, x * 4 + y].astype(F32)
    for k in range(31):
        mine = mine + c1_r[k].astype(F32)
    c2_s[...] = mine.astype(BF)
    for dz in (4, 3, 5, 2, 6, 1, 7):
        send(c2_s, c2_r.at[dz - 1], ST_C2, along_z(dz))
    arrived(b2_r, ST_B2)
    for k in range(3):
        block = block + b2_r[k].astype(F32)
    si[y] = block.astype(BF)
    for k in (2, 1, 3):
        send(si.at[y], si.at[y], ST_B3, in_plane(0, k))

    arrived(c2_r, ST_C2)
    for k in range(7):
        mine = mine + c2_r[k].astype(F32)
    rs[core, x * 4 + y] = mine.astype(BF)
    for dx, dc, dy in third:
        send(
            rs.at[core, x * 4 + y],
            rs.at[core, x * 4 + y],
            ST_C3,
            across(dx, dc, dy),
        )
    for h in range(2):
        joint[:, 256 * h : 256 * h + 256] = nn(
            bd[:, 384:], d1[:, 256 + 256 * h : 512 + 256 * h]
        ).astype(BF)
    arrived(bi_r, ST_B3)
    second_iface = jnp.concatenate([si[j] for j in range(4)], axis=1)
    pre_mid[...] = nt(second_iface, d2[:, :512])
    arrived(c1_r, ST_C3)
    top = jnp.zeros((R, 64), F32)
    for j in range(16):
        v = jnp.concatenate([rs[0, j].astype(F32), rs[1, j].astype(F32)], axis=0)
        top = top + nt(v.astype(BF), dr[:, 384 * j : 384 * j + 384])
    d_all[here] = jnp.concatenate([top[:8], top[8:]], axis=1).astype(BF)
    for dz, dy in plane:
        send(d_all.at[here], d_all.at[here], ST_D, in_plane(dz, dy))
    arrived(b_r, ST_D)
    top_bound = jnp.concatenate(
        [unpack(d_all[2 * j], d_all[2 * j + 1]) for j in range(8)], axis=1
    )
    e_all[y] = (pre_mid[...] + nt(top_bound, d2[:, 512:])).astype(BF)
    for k in (2, 1, 3):
        send(e_all.at[y], e_all.at[y], ST_E, in_plane(0, k))
    arrived(a_r, ST_E)
    mid_bound = jnp.concatenate([e_all[j] for j in range(4)], axis=1)
    lb_ref[...] = (pre_leaf[...] + nt(mid_bound, joint[...])).astype(BF)

    sent(a_r, ST_A)
    sent(ai_r, ST_AI)
    sent(b_r, ST_B)
    sent(bi_r, ST_BI)
    sent(b2_r, ST_B2)
    sent(bi_r, ST_B3)
    sent(c1_r, ST_C1)
    sent(c2_r, ST_C2)
    sent(c1_r, ST_C3)
    sent(b_r, ST_D)
    sent(a_r, ST_E)


def lift(lb_ref, part_ref, ll_ref, out_ref):
    low = lax.broadcasted_iota(jnp.int32, (R, 128), 1) < 64
    zero = jnp.zeros((R, 128), BF)
    for m in range(8):
        pair = lb_ref[:, 128 * m : 128 * m + 128]
        both = jnp.concatenate(
            [jnp.where(low, pair, zero), jnp.where(low, zero, pair)], axis=0
        )
        lifted = nn(both, ll_ref[128 * m : 128 * m + 128, :])
        out_ref[:, 2 * m, :] = lifted[:16] + part_ref[2 * m]
        out_ref[:, 2 * m + 1, :] = lifted[16:] + part_ref[2 * m + 1]


def per_device(src, lf, lp, ll, bu, bd, u1, d1, u2, d2, ur, dr):
    args = (src, lf, lp, bu, bd, u1, d1, u2, d2, ur, dr)
    vmem = pl.BlockSpec(memory_space=pltpu.VMEM)
    lb, part = pl.pallas_call(
        kernel,
        out_shape=(
            jax.ShapeDtypeStruct((R, 1024), BF),
            jax.ShapeDtypeStruct((LEAF, R, 256), F32),
        ),
        in_specs=[pl.BlockSpec(memory_space=pltpu.HBM)] * 11,
        out_specs=(vmem, vmem),
        scratch_shapes=[pltpu.VMEM(a.shape, BF) for a in args]
        + [
            pltpu.VMEM((256, 256), BF),
            pltpu.VMEM((16, 1024), F32),
            pltpu.VMEM((16, 128), F32),
            pltpu.VMEM((1024, 512), BF),
            pltpu.VMEM((4, 16, 128), BF),
            pltpu.VMEM((3, 16, 128), BF),
            pltpu.VMEM((16, 256), BF),
            pltpu.VMEM((3, 16, 256), BF),
            pltpu.VMEM((16, 8, 128), BF),
            pltpu.VMEM((15, 8, 128), BF),
            pltpu.VMEM((4, 16, 128), BF),
            pltpu.VMEM((3, 16, 128), BF),
            pltpu.VMEM((16, 128), BF),
            pltpu.VMEM((3, 16, 128), BF),
            pltpu.VMEM((4, 16, 128), BF),
            pltpu.VMEM((2, 16, 8, 384), BF),
            pltpu.VMEM((31, 8, 384), BF),
            pltpu.VMEM((8, 384), BF),
            pltpu.VMEM((7, 8, 384), BF),
            pltpu.VMEM((2, 16, 8, 384), BF),
            pltpu.VMEM((16, 8, 128), BF),
            pltpu.VMEM((4, 16, 128), BF),
            pltpu.SemaphoreType.DMA((12,)),
            pltpu.SemaphoreType.DMA((N_STAGE,)),
            pltpu.SemaphoreType.DMA((N_STAGE,)),
        ],
        compiler_params=pltpu.CompilerParams(
            collective_id=0, has_side_effects=True, vmem_limit_bytes=32 * 1024 * 1024
        ),
    )(*[pltpu.with_memory_space_constraint(a, pltpu.HBM) for a in args])
    return pl.pallas_call(
        lift,
        out_shape=jax.ShapeDtypeStruct((R, LEAF, 256), F32),
        in_specs=[vmem] * 3,
        out_specs=vmem,
        compiler_params=pltpu.CompilerParams(vmem_limit_bytes=8 * 1024 * 1024),
    )(lb, part, ll)


def solution(mesh):
    both = ("gx", "gy")
    return jax.shard_map(
        per_device,
        mesh=mesh,
        in_specs=(P(None, both, None),) + (P(both, None),) * 11,
        out_specs=P(None, both, None),
        check_vma=False,
    )
```
